32 devices in a mesh: groups: 2 (over y), band: 4 (over z), head: 4 (over x, core).
Axes of the slice: x: 2, y: 2, z: 4, core: 2. Of those that a mesh axis runs over, the one named last changes fastest.
Arguments:
- latent: bfloat16 [24, 128, 1280], P(('groups', 'band'), None, 'head'), parts along dimension 0, may hold values from -80 to 80
- first_gain: float32 [1280], P('head'), may hold values from 0.1 to 1.9
- first_shift: float32 [1280], P('head'), may hold values from -3 to 3
- kernel: bfloat16 [1280, 3, 3, 1280], P('head'), may hold values from -0.0546875 to 0.0546875
- kernel_bias: float32 [1280], P('head'), may hold values from -3 to 3
- second_gain: float32 [1280], P('head'), may hold values from 0.1 to 1.9
- second_shift: float32 [1280], P('head'), may hold values from -3 to 3
- projection: bfloat16 [1280, 3, 1024], P('band', None, 'head'), may hold values from -0.8385255 to 0.8385255
- output_weight: bfloat16 [1280, 1024], P('head'), may hold values from -0.1875 to 0.1875
- output_bias: float32 [1280], P('head'), may hold values from -3 to 3
Outputs:
- convolved: bfloat16 [24, 128, 1280], P(('groups', 'band'), None, 'head'), parts along dimension 0
- attended: bfloat16 [24, 128, 1280], P(('groups', 'band'), None, 'head'), parts along dimension 0
The draws below stay inside these ranges and needn't reach their ends.
There are 2 independent parts, one for each index of `groups`. The reference program is written for one: setup_inputs(seed, part) draws one part's arguments, and reference() takes and returns one part's arrays. A program takes and returns all parts, laid end to end along the dimension named above; an argument that names none is the same for every part. Nothing has to cross between parts.
All inputs are finite; a program needn't handle non-finite values.
Results may differ from the reference program's by a relative error of at most 0.012.
Values may be sent and summed in bfloat16 or wider, within the bound.
A program may use at most 128 MiB of HBM per device.

```python
import math
import jax
import jax.numpy as jnp
from jax import lax

CHANNELS = 1280
HEADS = 16
HEAD_SIZE = 64
NORM_GROUPS = 32
WIDTH = 128
HEIGHT = 12
INNER = 1024


def draw_latent(key, part):
    first, second = jax.random.split(key, 2)
    place = jnp.arange(HEIGHT).astype(jnp.float32) / max(HEIGHT - 1, 1)
    channel_scale = jnp.exp(jax.random.uniform(second, (CHANNELS,), minval=math.log(0.25), maxval=math.log(2.5)))
    row_scale = jnp.exp(place * math.log(3.0))
    base = jnp.clip(jax.random.normal(first, (HEIGHT, WIDTH, CHANNELS)), -4.0, 4.0)
    return (base * row_scale[:, None, None] * channel_scale).astype(jnp.bfloat16)


def draw_projection(key, part):
    first = jax.random.fold_in(key, 0)
    base = jnp.clip(jax.random.normal(first, (CHANNELS, 3, INNER)), -5.0, 5.0)
    factor = jnp.array([1.3, 1.3, 1.0], jnp.float32)[:, None] * jnp.ones((1, INNER), jnp.float32)
    return (base * factor[None] / math.sqrt(CHANNELS)).astype(jnp.bfloat16)


def block_scale(stream_key, dims, cuts, least, largest):
    level = 1.0
    for dim, shards_of in cuts:
        draws = jax.random.uniform(jax.random.fold_in(jax.random.fold_in(stream_key, 6), dim), (shards_of,), jnp.float32, least / len(cuts), largest / len(cuts))
        level = level * jnp.repeat(jnp.exp(draws), dims[dim] // shards_of).reshape((-1,) + (1,) * (len(dims) - 1 - dim))
    return level


def normal_values(rng, dims, deviation, limit, shards=(), dtype=jnp.bfloat16):
    drawn = jax.random.normal(rng, dims, jnp.float32) * deviation
    if len(shards) > 0:
        drawn = block_scale(rng, dims, shards, -0.22, 0.18) * drawn
    return jnp.clip(drawn, min=-limit, max=limit).astype(dtype)


def setup_inputs(seed: int = 0, part: int = 0) -> dict:
    key_of = jax.random.split(jax.random.key(seed), 11)
    own_keys = jax.random.split(jax.random.fold_in(key_of[10], part), 11)
    return {
        "latent": draw_latent(jax.random.fold_in(jax.random.fold_in(key_of[10], part), 71), part),
        "first_gain": jnp.clip(1.0 + 0.18 * jax.random.normal(key_of[1], (CHANNELS,), jnp.float32), 0.1, 1.9),
        "first_shift": normal_values(key_of[2], (CHANNELS,), 0.5, 3.0, ((0, 4),), jnp.float32),
        "kernel": normal_values(key_of[3], (CHANNELS, 3, 3, CHANNELS), (9 * CHANNELS) ** -0.5, 0.0546875, ((0, 4),)),
        "kernel_bias": normal_values(key_of[4], (CHANNELS,), 0.5, 3.0, ((0, 4),), jnp.float32),
        "second_gain": jnp.clip(1.0 + 0.18 * jax.random.normal(key_of[5], (CHANNELS,), jnp.float32), 0.1, 1.9),
        "second_shift": normal_values(key_of[6], (CHANNELS,), 0.5, 3.0, ((0, 4),), jnp.float32),
        "projection": draw_projection(jax.random.fold_in(key_of[10], 71), part),
        "output_weight": normal_values(key_of[8], (CHANNELS, INNER), INNER ** -0.5, 0.1875, ((0, 4),)),
        "output_bias": normal_values(key_of[9], (CHANNELS,), 0.5, 3.0, ((0, 4),), jnp.float32),
    }


def group_norm(values, gain, shift):
    height, width, channels = values.shape
    grouped = values.reshape(height * width, NORM_GROUPS, channels // NORM_GROUPS)
    mean = lax.optimization_barrier(jnp.mean(grouped, axis=(0, 2)))
    centered = grouped - mean[None, :, None]
    spread = lax.optimization_barrier(jnp.mean(centered * centered, axis=(0, 2)))
    scaled = centered / jnp.sqrt(spread + 1e-05)[None, :, None]
    return scaled.reshape(height, width, channels) * gain + shift

def one_head(operands):
    query, keys, values = operands
    scores = jnp.dot(query, keys.T, preferred_element_type=jnp.float32) * HEAD_SIZE ** (-0.5)
    top = lax.optimization_barrier(jnp.max(scores, axis=1, keepdims=True))
    weights = jnp.exp(scores - top)
    total = lax.optimization_barrier(jnp.sum(weights, axis=1, keepdims=True))
    mixed = jnp.dot(weights.astype(jnp.bfloat16), values, preferred_element_type=jnp.float32)
    return mixed / total

def reference(latent, first_gain, first_shift, kernel, kernel_bias, second_gain, second_shift, projection, output_weight, output_bias):
    latent_wide = latent.astype(jnp.float32)
    activated = jax.nn.silu(group_norm(latent_wide, first_gain, first_shift)).astype(jnp.bfloat16)
    padded = jnp.pad(activated, ((1, 1), (1, 1), (0, 0)))
    summed = jnp.zeros((HEIGHT * WIDTH, CHANNELS), jnp.float32)
    for above in range(3):
        for beside in range(3):
            window = padded[above:above + HEIGHT, beside:beside + WIDTH, :].reshape(HEIGHT * WIDTH, CHANNELS)
            summed = summed + jnp.dot(window, kernel[:, above, beside, :].T, preferred_element_type=jnp.float32)
    convolved = (latent_wide + kernel_bias + summed.reshape(HEIGHT, WIDTH, CHANNELS)).astype(jnp.bfloat16)
    normed = group_norm(convolved.astype(jnp.float32), second_gain, second_shift).astype(jnp.bfloat16)
    tokens = normed.reshape(HEIGHT * WIDTH, CHANNELS)
    projected = jnp.dot(tokens, projection.reshape(CHANNELS, 3 * INNER), preferred_element_type=jnp.float32)
    projected = projected.astype(jnp.bfloat16).reshape(HEIGHT * WIDTH, 3, HEADS, HEAD_SIZE)
    query = jnp.transpose(projected[:, 0], (1, 0, 2))
    keys = jnp.transpose(projected[:, 1], (1, 0, 2))
    values = jnp.transpose(projected[:, 2], (1, 0, 2))
    heads_out = lax.map(one_head, (query, keys, values))
    attention = jnp.transpose(heads_out, (1, 0, 2)).reshape(HEIGHT * WIDTH, INNER).astype(jnp.bfloat16)
    outgoing = jnp.dot(attention, output_weight.T, preferred_element_type=jnp.float32)
    attended = convolved.astype(jnp.float32).reshape(HEIGHT * WIDTH, CHANNELS) + output_bias + outgoing
    return (convolved, attended.reshape(HEIGHT, WIDTH, CHANNELS).astype(jnp.bfloat16))
```

```python
import functools
import math

import jax
import jax.numpy as jnp
from jax import lax
from jax.experimental import pallas as pl
from jax.experimental.pallas import tpu as pltpu
from jax.sharding import PartitionSpec as P

CHANNELS = 1280
HEADS = 16
HEAD_SIZE = 64
NORM_GROUPS = 32


def padded_2(cells, sides, width):
    for axis, dim in sides:
        count = lax.axis_size(axis)
        ends = count - 1
        head = lax.slice_in_dim(cells, 0, width, axis=dim)
        tail = lax.slice_in_dim(cells, cells.shape[dim] - width, cells.shape[dim], axis=dim)
        cells = jnp.concatenate(
            [
                lax.ppermute(tail, axis, [(i, (i + 1) % count) for i in range(ends)]),
                cells,
                lax.ppermute(head, axis, [((i + 1) % count, i) for i in range(ends)]),
            ],
            axis=dim,
        )
    return cells


def normalize(values, gain, shift, group_width, count):
    band_rows, width, channels = values.shape
    grouped = values.reshape(band_rows * width, channels // group_width, group_width)
    mean = lax.psum(jnp.sum(grouped, axis=(0, 2)), "band") / count
    centered = grouped - mean[None, :, None]
    spread = lax.psum(jnp.sum(centered * centered, axis=(0, 2)), "band") / count
    scaled = centered * lax.rsqrt(spread + 1e-05)[None, :, None]
    return scaled.reshape(band_rows, width, channels) * gain + shift


def contract_last(left, right):
    return lax.dot_general(
        left, right, (((1,), (1,)), ((), ())), preferred_element_type=jnp.float32
    )


def kernel_block(padded, weights, band_rows, width):
    inputs = padded.shape[2]
    wide = jnp.pad(padded, ((0, 0), (1, 1), (0, 0)))
    summed = jnp.zeros((band_rows * width, weights.shape[0]), jnp.float32)
    for above in range(3):
        for beside in range(3):
            window = wide[above : above + band_rows, beside : beside + width, :].reshape(
                band_rows * width, inputs
            )
            summed = summed + contract_last(window, weights[:, above, beside, :])
    return summed


def shards(
    latent,
    first_gain,
    first_shift,
    kernel,
    kernel_bias,
    second_gain,
    second_shift,
    projection,
    output_weight,
    output_bias,
):
    band_rows, width, channels = latent.shape
    tokens = band_rows * width
    group_width = CHANNELS // NORM_GROUPS
    count = lax.axis_size("band") * band_rows * width * group_width
    outputs = kernel.shape[0]
    latent_wide = latent.astype(jnp.float32)
    activated = jax.nn.silu(
        normalize(latent_wide, first_gain, first_shift, group_width, count)
    ).astype(jnp.bfloat16)
    gathered = lax.all_gather(activated, "head", axis=2, tiled=True)
    padded = padded_2(gathered, (("band", 0),), 1)
    summed = kernel_block(padded, kernel, band_rows, width)
    convolved = (latent_wide + kernel_bias + summed.reshape(band_rows, width, outputs)).astype(
        jnp.bfloat16
    )
    normed = normalize(
        convolved.astype(jnp.float32), second_gain, second_shift, group_width, count
    ).astype(jnp.bfloat16)
    features = lax.all_gather(normed, "head", axis=2, tiled=True).reshape(tokens, CHANNELS)
    local_inner = projection.shape[2]
    local_heads = local_inner // HEAD_SIZE
    piece = lax.all_gather(projection, "band", axis=0, tiled=True)
    projected = jnp.dot(
        features, piece.reshape(piece.shape[0], 3 * local_inner), preferred_element_type=jnp.float32
    )
    projected = projected.astype(jnp.bfloat16).reshape(tokens, 3, local_inner)
    query = projected[:, 0].reshape(tokens, local_heads, HEAD_SIZE)
    key_value = projected[:, 1:]
    factor = HEAD_SIZE ** (-0.5)
    piece = lax.all_gather(key_value, "band", axis=0, tiled=True)
    running = jnp.full((local_heads, tokens), -1e30, jnp.float32)
    keys = piece[:, 0].reshape(piece.shape[0], local_heads, HEAD_SIZE)
    values = piece[:, 1].reshape(piece.shape[0], local_heads, HEAD_SIZE)
    scores = jnp.einsum("qhd,khd->hqk", query, keys, preferred_element_type=jnp.float32) * factor
    highest = jnp.maximum(running, jnp.max(scores, axis=2))
    weights = jnp.exp(scores - highest[:, :, None])
    total = jnp.sum(weights, axis=2)
    summed_values = jnp.einsum(
        "hqk,khd->hqd", weights.astype(jnp.bfloat16), values, preferred_element_type=jnp.float32
    )
    running, total, summed_values = (highest, total, summed_values)
    attention = (
        jnp.transpose(summed_values / total[:, :, None], (1, 0, 2))
        .reshape(tokens, local_inner)
        .astype(jnp.bfloat16)
    )
    outgoing = contract_last(lax.all_gather(attention, "head", axis=1, tiled=True), output_weight)
    attended = (
        convolved.astype(jnp.float32) + output_bias + outgoing.reshape(band_rows, width, outputs)
    )
    return (convolved, attended.astype(jnp.bfloat16))


def pair_kernel(
    shape,
    lat_ref,
    prm_ref,
    kw_hbm,
    pj_hbm,
    ow_hbm,
    conv_ref,
    att_ref,
    kw,
    pw,
    ow,
    stat_a,
    stat_b,
    grid_in,
    norm_in,
    qkv_out,
    qkv_in,
    att_out,
    att_in,
    local_sem,
    send_sem,
    recv_sem,
):
    parts, bands, heads, rows, local, width = shape
    channels = local * heads
    tokens = rows * width
    groups_here = local // (CHANNELS // NORM_GROUPS)
    group_width = local // groups_here
    g, b, h = lax.axis_index("groups"), lax.axis_index("band"), lax.axis_index("head")
    sibling = h + 1 - 2 * lax.rem(h, 2)
    cross = lax.rem(h + 2, heads)
    far = lax.rem(sibling + 2, heads)
    used = [0]

    def remote(src, dst, groups=None, band=None, head=None):
        index = used[0]
        used[0] += 1
        return pltpu.make_async_remote_copy(
            src_ref=src,
            dst_ref=dst,
            send_sem=send_sem.at[index],
            recv_sem=recv_sem.at[index],
            device_id=(
                g if groups is None else groups,
                b if band is None else band,
                h if head is None else head,
            ),
            device_id_type=pl.DeviceIdType.MESH,
        )

    opened = []

    def begin(copy, sends=None):
        opened.append((copy, sends))
        if sends is None:
            copy.start()
        else:

            @pl.when(sends)
            def _():
                copy.start()

    def channel_rows(shard):
        return pl.ds(pl.multiple_of(shard * local, local), local)

    band_peers = [lax.rem(b + step, bands) for step in range(1, bands)]
    band_sources = [lax.rem(b - step + bands, bands) for step in range(1, bands)]
    part_peers = [lax.rem(g + step, parts) for step in range(1, parts)]
    part_sources = [lax.rem(g - step + parts, parts) for step in range(1, parts)]

    load_kernel = pltpu.make_async_copy(kw_hbm, kw, local_sem.at[0])
    load_output = pltpu.make_async_copy(ow_hbm, ow, local_sem.at[1])
    load_rows = pltpu.make_async_copy(pj_hbm, pw.at[:, channel_rows(b), :], local_sem.at[2])
    load_kernel.start()
    load_output.start()
    load_rows.start()

    barrier = pltpu.get_barrier_semaphore()
    neighbours = (
        [(g, b, sibling), (g, b, cross)]
        + [(g, peer, h) for peer in band_peers]
        + [(peer, b, h) for peer in part_peers]
    )
    for neighbour in neighbours:
        pl.semaphore_signal(
            barrier, inc=1, device_id=neighbour, device_id_type=pl.DeviceIdType.MESH
        )

    def statistics(read, stat):
        values = [
            read(row).astype(jnp.float32).reshape(groups_here, group_width, width)
            for row in range(rows)
        ]
        count = rows * width * group_width
        total = sum(jnp.sum(value, axis=1) for value in values)
        mean = jnp.sum(total, axis=1, keepdims=True) / count
        mean = jnp.broadcast_to(mean, (groups_here, width))
        squares = 0.0
        for value in values:
            centered = value - mean[:, None, :]
            squares = squares + jnp.sum(centered * centered, axis=1)
        squares = jnp.sum(squares, axis=1, keepdims=True)
        stat[b, 0] = mean
        stat[b, 1] = jnp.broadcast_to(squares, (groups_here, width))

    def exchange(stat):
        return [remote(stat.at[b], stat.at[b], band=peer) for peer in band_peers]

    def combined(stat):
        count = rows * width * group_width
        means = [stat[index, 0] for index in range(bands)]
        mean = sum(means) / bands
        spread = 0.0
        for index in range(bands):
            offset = means[index] - mean
            spread = spread + (stat[index, 1] + offset * offset * count)
        return mean, lax.rsqrt(spread / (count * bands) + 1e-05)

    def normalized(value, mean, scale, gain, shift):
        grouped = value.astype(jnp.float32).reshape(groups_here, group_width, width)
        scaled = (grouped - mean[:, None, :]) * scale[:, None, :]
        return scaled.reshape(local, width) * gain + shift

    params = prm_ref[...]
    padded = jnp.concatenate(
        [params, jnp.zeros((128 - params.shape[0], params.shape[1]), jnp.float32)], axis=0
    )
    columns = padded.T
    column = lambda index: columns[:local, index : index + 1]

    statistics(lambda row: lat_ref[row], stat_a)
    pl.semaphore_wait(barrier, len(neighbours))
    first = exchange(stat_a)
    for copy in first:
        begin(copy)
    for copy in first:
        copy.wait_recv()

    mean, scale = combined(stat_a)
    mine, crossed, sibs, fars = (channel_rows(s) for s in (h, cross, sibling, far))
    for row in range(rows):
        value = normalized(lat_ref[row], mean, scale, column(0), column(1))
        grid_in[row + 1, mine, :] = (value / (1.0 + jnp.exp(-value))).astype(jnp.bfloat16)

    def gather_pieces(buffer, pieces):
        sent = []
        for piece in pieces:
            own = buffer.at[piece, mine, :]
            there = buffer.at[piece, crossed, :]
            sent.append(
                (
                    remote(own, own, head=cross),
                    remote(own, own, head=sibling),
                    remote(there, there, head=sibling),
                )
            )
        return sent

    edges = (pl.ds(rows, 1), pl.ds(1, 1), pl.ds(2, rows - 2))
    gathered = gather_pieces(grid_in, edges)
    below, above = lax.rem(b + 1, bands), lax.rem(b + bands - 1, bands)
    halo = []
    for source, target, peer, sends, receives in (
        (rows, 0, below, b < bands - 1, b > 0),
        (1, rows + 1, above, b > 0, b < bands - 1),
    ):
        for shard in (mine, crossed):
            move = remote(grid_in.at[source, shard, :], grid_in.at[target, shard, :], band=peer)
            onward = grid_in.at[target, shard, :]
            halo.append((move, remote(onward, onward, head=sibling), sends, receives))
    for to_cross, to_sibling, _ in gathered:
        begin(to_cross)
        begin(to_sibling)
    for index in (0, 2):
        move, _, sends, _ = halo[index]
        begin(move, sends)

    share = local // parts

    def share_rows(band, part):
        return pl.ds(pl.multiple_of(band * local + part * share, share), share)

    weights = [
        remote(
            pj_hbm.at[:, pl.ds(pl.multiple_of(g * share, share), share), :],
            pw.at[:, share_rows(b, g), :],
            band=peer,
        )
        for peer in band_peers
    ]
    for index, (to_cross, _, onward) in enumerate(gathered):
        to_cross.wait_recv()
        begin(onward)
        if index < 2:
            move, _, sends, _ = halo[2 * index + 1]
            begin(move, sends)

    for copy in weights:
        begin(copy)

    for target, receives in ((0, b > 0), (rows + 1, b < bands - 1)):

        @pl.when(jnp.logical_not(receives))
        def _(target=target):
            grid_in[target] = jnp.zeros((channels, width), jnp.bfloat16)

    for move, onward, _, receives in halo:

        @pl.when(receives)
        def _(move=move):
            move.wait_recv()

        begin(onward, receives)

    for _, to_sibling, onward in gathered:
        to_sibling.wait_recv()
        onward.wait_recv()
    for _, onward, _, receives in halo:

        @pl.when(receives)
        def _(onward=onward):
            onward.wait_recv()

    load_kernel.wait()
    taps = []
    for beside in range(3):
        summed = None
        for over in range(3):
            window = jnp.concatenate([grid_in[over + row] for row in range(rows)], axis=1)
            part = jnp.dot(kw[over, beside], window, preferred_element_type=jnp.float32)
            summed = part if summed is None else summed + part
        taps.append(summed)
    place = lax.broadcasted_iota(jnp.int32, (local, width), 1)
    bias = column(2)
    for row in range(rows):
        span = slice(row * width, (row + 1) * width)
        left = jnp.where(place == 0, 0.0, pltpu.roll(taps[0][:, span], 1, 1))
        right = jnp.where(place == width - 1, 0.0, pltpu.roll(taps[2][:, span], width - 1, 1))
        value = lat_ref[row].astype(jnp.float32) + bias + (taps[1][:, span] + left + right)
        conv_ref[row] = value.astype(jnp.bfloat16)

    statistics(lambda row: conv_ref[row], stat_b)
    second = exchange(stat_b)
    for copy in second:
        begin(copy)

    passed = []
    for copy, source in zip(weights, band_sources):
        copy.wait_recv()
        onward = pw.at[:, share_rows(source, g), :]
        for peer in part_peers:
            move = remote(onward, onward, groups=peer)
            begin(move)
            passed.append(move)

    for copy in second:
        copy.wait_recv()
    mean, scale = combined(stat_b)
    for row in range(rows):
        value = normalized(conv_ref[row], mean, scale, column(3), column(4))
        norm_in[row, mine, :] = value.astype(jnp.bfloat16)
    normed = gather_pieces(norm_in, (pl.ds(0, rows),))
    for to_cross, to_sibling, onward in normed:
        begin(to_cross)
        begin(to_sibling)
        to_cross.wait_recv()
        begin(onward)
    load_rows.wait()
    for move in passed:
        move.wait_recv()
    for to_cross, to_sibling, onward in normed:
        to_sibling.wait_recv()
        onward.wait_recv()

    features = jnp.concatenate([norm_in[row] for row in range(rows)], axis=1)
    contract_first = lambda left, right: lax.dot_general(
        left, right, (((0,), (0,)), ((), ())), preferred_element_type=jnp.float32
    )
    for kind in range(3):
        made = contract_first(pw[kind], features).astype(jnp.bfloat16)
        for head in range(bands):
            qkv_out[head, kind * HEAD_SIZE : (kind + 1) * HEAD_SIZE, :] = made[
                head * HEAD_SIZE : (head + 1) * HEAD_SIZE
            ]
    spread = [remote(qkv_out.at[peer], qkv_in.at[b], band=peer) for peer in band_peers]
    for copy in spread:
        begin(copy)
    qkv_in[b] = qkv_out[b]
    for copy in spread:
        copy.wait_recv()

    keys = jnp.concatenate([qkv_in[s, HEAD_SIZE : 2 * HEAD_SIZE, :] for s in range(bands)], axis=1)
    values = jnp.concatenate([qkv_in[s, 2 * HEAD_SIZE :, :] for s in range(bands)], axis=1)
    keys = keys.T
    inner = bands * HEAD_SIZE
    feature_rows = lambda shard: pl.ds(pl.multiple_of(shard * inner, inner), inner)
    my_head = pl.ds(pl.multiple_of(h * inner + b * HEAD_SIZE, HEAD_SIZE), HEAD_SIZE)
    factor = HEAD_SIZE ** (-0.5) * math.log2(math.e)
    returned = [
        remote(att_out.at[step], att_in.at[my_head, :], band=peer)
        for step, peer in enumerate(band_peers)
    ]
    for step in range(1, bands + 1):
        peer = lax.rem(b + step, bands)
        query = qkv_in[peer, :HEAD_SIZE, :]
        scores = jnp.dot(keys, query, preferred_element_type=jnp.float32)
        top = jnp.max(scores, axis=0, keepdims=True)
        heavy = jnp.exp2((scores - top) * factor)
        total = jnp.sum(heavy, axis=0, keepdims=True)
        mixed = jnp.dot(values, heavy.astype(jnp.bfloat16), preferred_element_type=jnp.float32)
        result = (mixed / total).astype(jnp.bfloat16)
        if step < bands:
            att_out[step - 1] = result
            begin(returned[step - 1])
        else:
            att_in[my_head, :] = result

    for copy in returned:
        copy.wait_recv()
    own, there = att_in.at[feature_rows(h), :], att_in.at[feature_rows(cross), :]
    to_cross = remote(own, own, head=cross)
    to_sibling = remote(own, own, head=sibling)
    onward = remote(there, there, head=sibling)
    begin(to_cross)
    begin(to_sibling)
    to_cross.wait_recv()
    begin(onward)
    load_output.wait()
    to_sibling.wait_recv()
    onward.wait_recv()
    outgoing = jnp.dot(ow[...], att_in[...], preferred_element_type=jnp.float32)
    bias = column(5)
    for row in range(rows):
        span = slice(row * width, (row + 1) * width)
        value = conv_ref[row].astype(jnp.float32) + bias + outgoing[:, span]
        att_ref[row] = value.astype(jnp.bfloat16)

    for copy, sends in opened:
        if sends is None:
            copy.wait_send()
        else:

            @pl.when(sends)
            def _(copy=copy):
                copy.wait_send()


def pair_shards(
    parts,
    bands,
    heads,
    latent,
    first_gain,
    first_shift,
    kernel,
    kernel_bias,
    second_gain,
    second_shift,
    projection,
    output_weight,
    output_bias,
):
    rows, width, local = latent.shape
    channels, tokens = local * heads, rows * width
    inner = projection.shape[2]
    groups_here = local // (CHANNELS // NORM_GROUPS)
    vectors = [first_gain, first_shift, kernel_bias, second_gain, second_shift, output_bias]
    params = jnp.pad(jnp.stack(vectors), ((0, 2), (0, -local % 128)))
    vmem = pl.BlockSpec(memory_space=pltpu.VMEM)
    hbm = pl.BlockSpec(memory_space=pl.ANY)
    result = jax.ShapeDtypeStruct((rows, local, width), jnp.bfloat16)
    copies = 64
    call = pl.pallas_call(
        functools.partial(pair_kernel, (parts, bands, heads, rows, local, width)),
        out_shape=(result, result),
        in_specs=[vmem, vmem, hbm, hbm, hbm],
        out_specs=(vmem, vmem),
        scratch_shapes=[
            pltpu.VMEM((3, 3, local, channels), jnp.bfloat16),
            pltpu.VMEM((3, channels, inner), jnp.bfloat16),
            pltpu.VMEM((local, inner * heads), jnp.bfloat16),
            pltpu.VMEM((bands, 2, groups_here, width), jnp.float32),
            pltpu.VMEM((bands, 2, groups_here, width), jnp.float32),
            pltpu.VMEM((rows + 2, channels, width), jnp.bfloat16),
            pltpu.VMEM((rows, channels, width), jnp.bfloat16),
            pltpu.VMEM((bands, 3 * HEAD_SIZE, tokens), jnp.bfloat16),
            pltpu.VMEM((bands, 3 * HEAD_SIZE, tokens), jnp.bfloat16),
            pltpu.VMEM((bands - 1, HEAD_SIZE, tokens), jnp.bfloat16),
            pltpu.VMEM((inner * heads, tokens), jnp.bfloat16),
            pltpu.SemaphoreType.DMA((3,)),
            pltpu.SemaphoreType.DMA((copies,)),
            pltpu.SemaphoreType.DMA((copies,)),
        ],
        compiler_params=pltpu.CompilerParams(
            collective_id=0, has_side_effects=True, vmem_limit_bytes=60 << 20
        ),
    )
    convolved, attended = call(
        jnp.transpose(latent, (0, 2, 1)),
        params,
        jnp.transpose(kernel, (1, 2, 0, 3)),
        jnp.transpose(projection, (1, 0, 2)),
        output_weight,
    )
    return jnp.transpose(convolved, (0, 2, 1)), jnp.transpose(attended, (0, 2, 1))


def solution(mesh):
    placed = (
        P(("groups", "band"), None, "head"),
        P("head"),
        P("head"),
        P("head", None, None, None),
        P("head"),
        P("head"),
        P("head"),
        P("band", None, "head"),
        P("head", None),
        P("head"),
    )
    parts, bands, heads = (mesh.shape[axis] for axis in ("groups", "band", "head"))
    paired = heads == 4 and bands > 1 and HEADS == heads * bands and CHANNELS % (16 * parts * heads) == 0
    body = functools.partial(pair_shards, parts, bands, heads) if paired else shards
    return jax.shard_map(
        body,
        mesh=mesh,
        in_specs=placed,
        out_specs=(P(("groups", "band"), None, "head"), P(("groups", "band"), None, "head")),
        check_vma=False,
    )
```

```python
import functools
import math

import jax
import jax.numpy as jnp
from jax import lax
from jax.experimental import pallas as pl
from jax.experimental.pallas import tpu as pltpu
from jax.sharding import PartitionSpec as P

CHANNELS = 1280
HEADS = 16
HEAD_SIZE = 64
NORM_GROUPS = 32


def padded_2(cells, sides, width):
    for axis, dim in sides:
        count = lax.axis_size(axis)
        ends = count - 1
        head = lax.slice_in_dim(cells, 0, width, axis=dim)
        tail = lax.slice_in_dim(cells, cells.shape[dim] - width, cells.shape[dim], axis=dim)
        cells = jnp.concatenate(
            [
                lax.ppermute(tail, axis, [(i, (i + 1) % count) for i in range(ends)]),
                cells,
                lax.ppermute(head, axis, [((i + 1) % count, i) for i in range(ends)]),
            ],
            axis=dim,
        )
    return cells


def normalize(values, gain, shift, group_width, count):
    band_rows, width, channels = values.shape
    grouped = values.reshape(band_rows * width, channels // group_width, group_width)
    mean = lax.psum(jnp.sum(grouped, axis=(0, 2)), "band") / count
    centered = grouped - mean[None, :, None]
    spread = lax.psum(jnp.sum(centered * centered, axis=(0, 2)), "band") / count
    scaled = centered * lax.rsqrt(spread + 1e-05)[None, :, None]
    return scaled.reshape(band_rows, width, channels) * gain + shift


def contract_last(left, right):
    return lax.dot_general(
        left, right, (((1,), (1,)), ((), ())), preferred_element_type=jnp.float32
    )


def kernel_block(padded, weights, band_rows, width):
    inputs = padded.shape[2]
    wide = jnp.pad(padded, ((0, 0), (1, 1), (0, 0)))
    summed = jnp.zeros((band_rows * width, weights.shape[0]), jnp.float32)
    for above in range(3):
        for beside in range(3):
            window = wide[above : above + band_rows, beside : beside + width, :].reshape(
                band_rows * width, inputs
            )
            summed = summed + contract_last(window, weights[:, above, beside, :])
    return summed


def shards(
    latent,
    first_gain,
    first_shift,
    kernel,
    kernel_bias,
    second_gain,
    second_shift,
    projection,
    output_weight,
    output_bias,
):
    band_rows, width, channels = latent.shape
    tokens = band_rows * width
    group_width = CHANNELS // NORM_GROUPS
    count = lax.axis_size("band") * band_rows * width * group_width
    outputs = kernel.shape[0]
    latent_wide = latent.astype(jnp.float32)
    activated = jax.nn.silu(
        normalize(latent_wide, first_gain, first_shift, group_width, count)
    ).astype(jnp.bfloat16)
    gathered = lax.all_gather(activated, "head", axis=2, tiled=True)
    padded = padded_2(gathered, (("band", 0),), 1)
    summed = kernel_block(padded, kernel, band_rows, width)
    convolved = (latent_wide + kernel_bias + summed.reshape(band_rows, width, outputs)).astype(
        jnp.bfloat16
    )
    normed = normalize(
        convolved.astype(jnp.float32), second_gain, second_shift, group_width, count
    ).astype(jnp.bfloat16)
    features = lax.all_gather(normed, "head", axis=2, tiled=True).reshape(tokens, CHANNELS)
    local_inner = projection.shape[2]
    local_heads = local_inner // HEAD_SIZE
    piece = lax.all_gather(projection, "band", axis=0, tiled=True)
    projected = jnp.dot(
        features, piece.reshape(piece.shape[0], 3 * local_inner), preferred_element_type=jnp.float32
    )
    projected = projected.astype(jnp.bfloat16).reshape(tokens, 3, local_inner)
    query = projected[:, 0].reshape(tokens, local_heads, HEAD_SIZE)
    key_value = projected[:, 1:]
    factor = HEAD_SIZE ** (-0.5)
    piece = lax.all_gather(key_value, "band", axis=0, tiled=True)
    running = jnp.full((local_heads, tokens), -1e30, jnp.float32)
    keys = piece[:, 0].reshape(piece.shape[0], local_heads, HEAD_SIZE)
    values = piece[:, 1].reshape(piece.shape[0], local_heads, HEAD_SIZE)
    scores = jnp.einsum("qhd,khd->hqk", query, keys, preferred_element_type=jnp.float32) * factor
    highest = jnp.maximum(running, jnp.max(scores, axis=2))
    weights = jnp.exp(scores - highest[:, :, None])
    total = jnp.sum(weights, axis=2)
    summed_values = jnp.einsum(
        "hqk,khd->hqd", weights.astype(jnp.bfloat16), values, preferred_element_type=jnp.float32
    )
    running, total, summed_values = (highest, total, summed_values)
    attention = (
        jnp.transpose(summed_values / total[:, :, None], (1, 0, 2))
        .reshape(tokens, local_inner)
        .astype(jnp.bfloat16)
    )
    outgoing = contract_last(lax.all_gather(attention, "head", axis=1, tiled=True), output_weight)
    attended = (
        convolved.astype(jnp.float32) + output_bias + outgoing.reshape(band_rows, width, outputs)
    )
    return (convolved, attended.astype(jnp.bfloat16))


def pair_kernel(
    shape,
    lat_ref,
    prm_ref,
    kw_hbm,
    pj_hbm,
    ow_hbm,
    wide_ref,
    gain_ref,
    kw,
    pw,
    ow,
    stat_a,
    stat_b,
    grid_in,
    norm_in,
    qkv_out,
    qkv_in,
    att_out,
    att_in,
    conv_ref,
    local_sem,
    send_sem,
    recv_sem,
):
    parts, bands, heads, rows, local, width = shape
    channels = local * heads
    tokens = rows * width
    groups_here = local // (CHANNELS // NORM_GROUPS)
    group_width = local // groups_here
    g, b, h = lax.axis_index("groups"), lax.axis_index("band"), lax.axis_index("head")
    sibling = h + 1 - 2 * lax.rem(h, 2)
    cross = lax.rem(h + 2, heads)
    far = lax.rem(sibling + 2, heads)
    used = [0]

    def remote(src, dst, groups=None, band=None, head=None):
        index = used[0]
        used[0] += 1
        return pltpu.make_async_remote_copy(
            src_ref=src,
            dst_ref=dst,
            send_sem=send_sem.at[index],
            recv_sem=recv_sem.at[index],
            device_id=(
                g if groups is None else groups,
                b if band is None else band,
                h if head is None else head,
            ),
            device_id_type=pl.DeviceIdType.MESH,
        )

    opened = []

    def begin(copy, sends=None):
        opened.append((copy, sends))
        if sends is None:
            copy.start()
        else:

            @pl.when(sends)
            def _():
                copy.start()

    def channel_rows(shard):
        return pl.ds(pl.multiple_of(shard * local, local), local)

    band_peers = [lax.rem(b + step, bands) for step in range(1, bands)]
    band_sources = [lax.rem(b - step + bands, bands) for step in range(1, bands)]
    part_peers = [lax.rem(g + step, parts) for step in range(1, parts)]
    part_sources = [lax.rem(g - step + parts, parts) for step in range(1, parts)]

    load_kernel = pltpu.make_async_copy(kw_hbm, kw, local_sem.at[0])
    load_output = pltpu.make_async_copy(ow_hbm, ow, local_sem.at[1])
    load_rows = pltpu.make_async_copy(pj_hbm, pw.at[:, channel_rows(b), :], local_sem.at[2])
    load_kernel.start()
    load_output.start()
    load_rows.start()

    barrier = pltpu.get_barrier_semaphore()
    neighbours = (
        [(g, b, sibling), (g, b, cross)]
        + [(g, peer, h) for peer in band_peers]
        + [(peer, b, h) for peer in part_peers]
    )
    for neighbour in neighbours:
        pl.semaphore_signal(
            barrier, inc=1, device_id=neighbour, device_id_type=pl.DeviceIdType.MESH
        )

    def statistics(read, stat):
        values = [
            read(row).astype(jnp.float32).reshape(groups_here, group_width, width)
            for row in range(rows)
        ]
        count = rows * width * group_width
        total = sum(jnp.sum(value, axis=1) for value in values)
        mean = jnp.sum(total, axis=1, keepdims=True) / count
        mean = jnp.broadcast_to(mean, (groups_here, width))
        squares = 0.0
        for value in values:
            centered = value - mean[:, None, :]
            squares = squares + jnp.sum(centered * centered, axis=1)
        squares = jnp.sum(squares, axis=1, keepdims=True)
        stat[b, 0] = mean
        stat[b, 1] = jnp.broadcast_to(squares, (groups_here, width))

    def exchange(stat):
        return [remote(stat.at[b], stat.at[b], band=peer) for peer in band_peers]

    def combined(stat):
        count = rows * width * group_width
        means = [stat[index, 0] for index in range(bands)]
        mean = sum(means) / bands
        spread = 0.0
        for index in range(bands):
            offset = means[index] - mean
            spread = spread + (stat[index, 1] + offset * offset * count)
        return mean, lax.rsqrt(spread / (count * bands) + 1e-05)

    def normalized(value, mean, scale, gain, shift):
        grouped = value.astype(jnp.float32).reshape(groups_here, group_width, width)
        scaled = (grouped - mean[:, None, :]) * scale[:, None, :]
        return scaled.reshape(local, width) * gain + shift

    params = prm_ref[...]
    lanes = params.shape[1]
    padded = jnp.concatenate(
        [params, jnp.zeros((lanes - params.shape[0], lanes), jnp.float32)], axis=0
    )
    columns = padded.T
    blocks = -(-local // lanes)

    def column(index):
        pieces = [columns[:, index * blocks + k : index * blocks + k + 1] for k in range(blocks)]
        return jnp.concatenate(pieces, axis=0)[:local]

    statistics(lambda row: lat_ref[row], stat_a)
    pl.semaphore_wait(barrier, len(neighbours))
    first = exchange(stat_a)
    for copy in first:
        begin(copy)

    share = local // parts

    def share_rows(band, part):
        return pl.ds(pl.multiple_of(band * local + part * share, share), share)

    weights = [
        remote(
            pj_hbm.at[:, pl.ds(pl.multiple_of(g * share, share), share), :],
            pw.at[:, share_rows(b, g), :],
            band=peer,
        )
        for peer in band_peers
    ]
    for copy in weights:
        begin(copy)
    for copy in first:
        copy.wait_recv()

    mean, scale = combined(stat_a)
    mine, crossed, sibs, fars = (channel_rows(s) for s in (h, cross, sibling, far))
    for row in range(rows):
        value = normalized(lat_ref[row], mean, scale, column(0), column(1))
        grid_in[row + 1, mine, :] = (value / (1.0 + jnp.exp(-value))).astype(jnp.bfloat16)

    def gather_pieces(buffer, pieces):
        sent = []
        for piece in pieces:
            own = buffer.at[piece, mine, :]
            there = buffer.at[piece, crossed, :]
            sent.append(
                (
                    remote(own, own, head=cross),
                    remote(own, own, head=sibling),
                    remote(there, there, head=sibling),
                )
            )
        return sent

    edges = (pl.ds(rows, 1), pl.ds(1, 1), pl.ds(2, rows - 2))
    gathered = gather_pieces(grid_in, edges)
    below, above = lax.rem(b + 1, bands), lax.rem(b + bands - 1, bands)
    halo = []
    for source, target, peer, sends, receives in (
        (rows, 0, below, b < bands - 1, b > 0),
        (1, rows + 1, above, b > 0, b < bands - 1),
    ):
        for shard in (mine, crossed):
            move = remote(grid_in.at[source, shard, :], grid_in.at[target, shard, :], band=peer)
            onward = grid_in.at[target, shard, :]
            halo.append((move, remote(onward, onward, head=sibling), sends, receives))
    for to_cross, to_sibling, _ in gathered:
        begin(to_cross)
        begin(to_sibling)
    for index in (0, 2):
        move, _, sends, _ = halo[index]
        begin(move, sends)

    for index, (to_cross, _, onward) in enumerate(gathered):
        to_cross.wait_recv()
        begin(onward)
        if index < 2:
            move, _, sends, _ = halo[2 * index + 1]
            begin(move, sends)

    for target, receives in ((0, b > 0), (rows + 1, b < bands - 1)):

        @pl.when(jnp.logical_not(receives))
        def _(target=target):
            grid_in[target] = jnp.zeros((channels, width), jnp.bfloat16)

    for move, onward, _, receives in halo:

        @pl.when(receives)
        def _(move=move):
            move.wait_recv()

        begin(onward, receives)

    for _, to_sibling, onward in gathered:
        to_sibling.wait_recv()
        onward.wait_recv()
    for _, onward, _, receives in halo:

        @pl.when(receives)
        def _(onward=onward):
            onward.wait_recv()

    passed = []
    for copy, source in zip(weights, band_sources):
        copy.wait_recv()
        onward = pw.at[:, share_rows(source, g), :]
        for peer in part_peers:
            move = remote(onward, onward, groups=peer)
            begin(move)
            passed.append(move)

    load_kernel.wait()
    taps = []
    for beside in range(3):
        summed = None
        for over in range(3):
            window = jnp.concatenate([grid_in[over + row] for row in range(rows)], axis=1)
            part = jnp.dot(kw[over, beside], window, preferred_element_type=jnp.float32)
            summed = part if summed is None else summed + part
        taps.append(summed)
    place = lax.broadcasted_iota(jnp.int32, (local, width), 1)
    bias = column(2)
    for row in range(rows):
        span = slice(row * width, (row + 1) * width)
        left = jnp.where(place == 0, 0.0, pltpu.roll(taps[0][:, span], 1, 1))
        right = jnp.where(place == width - 1, 0.0, pltpu.roll(taps[2][:, span], width - 1, 1))
        value = lat_ref[row].astype(jnp.float32) + bias + (taps[1][:, span] + left + right)
        wide_ref[row] = value
        conv_ref[row] = value.astype(jnp.bfloat16)

    statistics(lambda row: conv_ref[row], stat_b)
    second = exchange(stat_b)
    for copy in second:
        begin(copy)

    for copy in second:
        copy.wait_recv()
    mean, scale = combined(stat_b)
    for row in range(rows):
        value = normalized(conv_ref[row], mean, scale, column(3), column(4))
        norm_in[row, mine, :] = value.astype(jnp.bfloat16)
    normed = gather_pieces(norm_in, (pl.ds(0, rows),))
    for to_cross, to_sibling, onward in normed:
        begin(to_cross)
        begin(to_sibling)
        to_cross.wait_recv()
        begin(onward)
    load_rows.wait()
    for move in passed:
        move.wait_recv()
    for to_cross, to_sibling, onward in normed:
        to_sibling.wait_recv()
        onward.wait_recv()

    features = jnp.concatenate([norm_in[row] for row in range(rows)], axis=1)
    contract_first = lambda left, right: lax.dot_general(
        left, right, (((0,), (0,)), ((), ())), preferred_element_type=jnp.float32
    )
    spread = []
    for kind in range(3):
        made = contract_first(pw[kind], features).astype(jnp.bfloat16)
        for head in range(bands):
            qkv_out[head, kind] = made[head * HEAD_SIZE : (head + 1) * HEAD_SIZE]
        qkv_in[b, kind] = qkv_out[b, kind]
        moves = [
            remote(qkv_out.at[peer, kind], qkv_in.at[b, kind], band=peer) for peer in band_peers
        ]
        for copy in moves:
            begin(copy)
        spread.append(moves)

    inner = bands * HEAD_SIZE
    factor = HEAD_SIZE ** (-0.5) * math.log2(math.e)

    def feature_rows(shard, band):
        return pl.ds(pl.multiple_of(shard * inner + band * HEAD_SIZE, HEAD_SIZE), HEAD_SIZE)

    sources = [b] + band_sources
    onwards = [lax.rem(b + step, bands) for step in range(bands)]
    queries, keys, values, running = [], [], [], []

    def attend(index, chunks):
        scores = [
            jnp.dot(keys[c], queries[index], preferred_element_type=jnp.float32) for c in chunks
        ]
        top = functools.reduce(
            jnp.maximum, [jnp.max(score, axis=0, keepdims=True) for score in scores]
        )
        before = running[index]
        if before is not None:
            top = jnp.maximum(top, before[0])
        total, mixed = 0.0, 0.0
        for c, score in zip(chunks, scores):
            heavy = jnp.exp2((score - top) * factor)
            total = total + jnp.sum(heavy, axis=0, keepdims=True)
            mixed = mixed + jnp.dot(
                values[c], heavy.astype(jnp.bfloat16), preferred_element_type=jnp.float32
            )
        if before is not None:
            fade = jnp.exp2((before[0] - top) * factor)
            total = total + before[1] * fade
            mixed = mixed + before[2] * fade
        running[index] = (top, total, mixed)

    def finished(index):
        _, total, mixed = running[index]
        return (mixed / total).astype(jnp.bfloat16)

    returned = [
        remote(att_out.at[index], att_in.at[feature_rows(h, b), :], band=source)
        for index, source in enumerate(band_sources)
    ]
    final = []
    for source in onwards:
        own = att_in.at[feature_rows(h, source), :]
        there = att_in.at[feature_rows(cross, source), :]
        final.append(
            (
                remote(own, own, head=cross),
                remote(own, own, head=sibling),
                remote(there, there, head=sibling),
            )
        )

    def pass_on(index):
        if index > 0:
            returned[index - 1].wait_recv()
        begin(final[index][0])
        begin(final[index][1])

    def relay(index):
        final[index][0].wait_recv()
        begin(final[index][2])

    for index in range(bands):
        if index > 0:
            for moves in spread:
                moves[index - 1].wait_recv()
        source = sources[index]
        queries.append(qkv_in[source, 0])
        keys.append(qkv_in[source, 1].T)
        values.append(qkv_in[source, 2])
        running.append(None)
        last = index == bands - 1
        for earlier in list(range(1, index)) + [index] + ([0] if index > 0 else []):
            attend(earlier, list(range(index + 1)) if earlier == index else [index])
            if last:
                if earlier > 0:
                    att_out[earlier - 1] = finished(earlier)
                    begin(returned[earlier - 1])
                else:
                    att_in[feature_rows(h, b), :] = finished(0)
    for index in range(bands):
        pass_on(index)
    for index in range(bands):
        relay(index)
    load_output.wait()
    for _, to_sibling, onward in final:
        to_sibling.wait_recv()
        onward.wait_recv()
    outgoing = jnp.dot(ow[...], att_in[...], preferred_element_type=jnp.float32)
    bias = column(5)
    for row in range(rows):
        span = slice(row * width, (row + 1) * width)
        gain_ref[row] = outgoing[:, span] + bias

    for copy, sends in opened:
        if sends is None:
            copy.wait_send()
        else:

            @pl.when(sends)
            def _(copy=copy):
                copy.wait_send()


def pair_shards(
    parts,
    bands,
    heads,
    latent,
    first_gain,
    first_shift,
    kernel,
    kernel_bias,
    second_gain,
    second_shift,
    projection,
    output_weight,
    output_bias,
):
    rows, width, local = latent.shape
    channels, tokens = local * heads, rows * width
    inner = projection.shape[2]
    groups_here = local // (CHANNELS // NORM_GROUPS)
    vectors = [first_gain, first_shift, kernel_bias, second_gain, second_shift, output_bias]
    gap = jnp.zeros((-local % 128,), jnp.float32)
    flat = jnp.concatenate([piece for vector in vectors for piece in (vector, gap)])
    params = jnp.pad(flat, (0, -flat.shape[0] % 1024)).reshape(-1, 128)
    vmem = pl.BlockSpec(memory_space=pltpu.VMEM)
    hbm = pl.BlockSpec(memory_space=pl.ANY)
    result = jax.ShapeDtypeStruct((rows, local, width), jnp.float32)
    copies = 64
    call = pl.pallas_call(
        functools.partial(pair_kernel, (parts, bands, heads, rows, local, width)),
        out_shape=(result, result),
        in_specs=[vmem, vmem, hbm, hbm, hbm],
        out_specs=(vmem, vmem),
        scratch_shapes=[
            pltpu.VMEM((3, 3, local, channels), jnp.bfloat16),
            pltpu.VMEM((3, channels, inner), jnp.bfloat16),
            pltpu.VMEM((local, inner * heads), jnp.bfloat16),
            pltpu.VMEM((bands, 2, groups_here, width), jnp.float32),
            pltpu.VMEM((bands, 2, groups_here, width), jnp.float32),
            pltpu.VMEM((rows + 2, channels, width), jnp.bfloat16),
            pltpu.VMEM((rows, channels, width), jnp.bfloat16),
            pltpu.VMEM((bands, 3, HEAD_SIZE, tokens), jnp.bfloat16),
            pltpu.VMEM((bands, 3, HEAD_SIZE, tokens), jnp.bfloat16),
            pltpu.VMEM((bands - 1, HEAD_SIZE, tokens), jnp.bfloat16),
            pltpu.VMEM((inner * heads, tokens), jnp.bfloat16),
            pltpu.VMEM((rows, local, width), jnp.bfloat16),
            pltpu.SemaphoreType.DMA((3,)),
            pltpu.SemaphoreType.DMA((copies,)),
            pltpu.SemaphoreType.DMA((copies,)),
        ],
        compiler_params=pltpu.CompilerParams(
            collective_id=0, has_side_effects=True, vmem_limit_bytes=60 << 20
        ),
    )
    wide, gained = call(
        jnp.transpose(latent, (0, 2, 1)),
        params,
        jnp.transpose(kernel, (1, 2, 0, 3)),
        jnp.transpose(projection, (1, 0, 2)),
        output_weight,
    )
    convolved = jnp.transpose(wide, (0, 2, 1)).astype(jnp.bfloat16)
    attended = convolved.astype(jnp.float32) + jnp.transpose(gained, (0, 2, 1))
    return convolved, attended.astype(jnp.bfloat16)


def solution(mesh):
    placed = (
        P(("groups", "band"), None, "head"),
        P("head"),
        P("head"),
        P("head", None, None, None),
        P("head"),
        P("head"),
        P("head"),
        P("band", None, "head"),
        P("head", None),
        P("head"),
    )
    parts, bands, heads = (mesh.shape[axis] for axis in ("groups", "band", "head"))
    paired = heads == 4 and bands > 1 and HEADS == heads * bands and CHANNELS % (16 * parts * heads) == 0
    body = functools.partial(pair_shards, parts, bands, heads) if paired else shards
    return jax.shard_map(
        body,
        mesh=mesh,
        in_specs=placed,
        out_specs=(P(("groups", "band"), None, "head"), P(("groups", "band"), None, "head")),
        check_vma=False,
    )
```

```python
import functools
import math

import jax
import jax.numpy as jnp
from jax import lax
from jax.experimental import pallas as pl
from jax.experimental.pallas import tpu as pltpu
from jax.sharding import PartitionSpec as P

CHANNELS = 1280
HEADS = 16
HEAD_SIZE = 64
NORM_GROUPS = 32


def padded_2(cells, sides, width):
    for axis, dim in sides:
        count = lax.axis_size(axis)
        ends = count - 1
        head = lax.slice_in_dim(cells, 0, width, axis=dim)
        tail = lax.slice_in_dim(cells, cells.shape[dim] - width, cells.shape[dim], axis=dim)
        cells = jnp.concatenate(
            [
                lax.ppermute(tail, axis, [(i, (i + 1) % count) for i in range(ends)]),
                cells,
                lax.ppermute(head, axis, [((i + 1) % count, i) for i in range(ends)]),
            ],
            axis=dim,
        )
    return cells


def normalize(values, gain, shift, group_width, count):
    band_rows, width, channels = values.shape
    grouped = values.reshape(band_rows * width, channels // group_width, group_width)
    mean = lax.psum(jnp.sum(grouped, axis=(0, 2)), "band") / count
    centered = grouped - mean[None, :, None]
    spread = lax.psum(jnp.sum(centered * centered, axis=(0, 2)), "band") / count
    scaled = centered * lax.rsqrt(spread + 1e-05)[None, :, None]
    return scaled.reshape(band_rows, width, channels) * gain + shift


def contract_last(left, right):
    return lax.dot_general(
        left, right, (((1,), (1,)), ((), ())), preferred_element_type=jnp.float32
    )


def kernel_block(padded, weights, band_rows, width):
    inputs = padded.shape[2]
    wide = jnp.pad(padded, ((0, 0), (1, 1), (0, 0)))
    summed = jnp.zeros((band_rows * width, weights.shape[0]), jnp.float32)
    for above in range(3):
        for beside in range(3):
            window = wide[above : above + band_rows, beside : beside + width, :].reshape(
                band_rows * width, inputs
            )
            summed = summed + contract_last(window, weights[:, above, beside, :])
    return summed


def shards(
    latent,
    first_gain,
    first_shift,
    kernel,
    kernel_bias,
    second_gain,
    second_shift,
    projection,
    output_weight,
    output_bias,
):
    band_rows, width, channels = latent.shape
    tokens = band_rows * width
    group_width = CHANNELS // NORM_GROUPS
    count = lax.axis_size("band") * band_rows * width * group_width
    outputs = kernel.shape[0]
    latent_wide = latent.astype(jnp.float32)
    activated = jax.nn.silu(
        normalize(latent_wide, first_gain, first_shift, group_width, count)
    ).astype(jnp.bfloat16)
    gathered = lax.all_gather(activated, "head", axis=2, tiled=True)
    padded = padded_2(gathered, (("band", 0),), 1)
    summed = kernel_block(padded, kernel, band_rows, width)
    convolved = (latent_wide + kernel_bias + summed.reshape(band_rows, width, outputs)).astype(
        jnp.bfloat16
    )
    normed = normalize(
        convolved.astype(jnp.float32), second_gain, second_shift, group_width, count
    ).astype(jnp.bfloat16)
    features = lax.all_gather(normed, "head", axis=2, tiled=True).reshape(tokens, CHANNELS)
    local_inner = projection.shape[2]
    local_heads = local_inner // HEAD_SIZE
    piece = lax.all_gather(projection, "band", axis=0, tiled=True)
    projected = jnp.dot(
        features, piece.reshape(piece.shape[0], 3 * local_inner), preferred_element_type=jnp.float32
    )
    projected = projected.astype(jnp.bfloat16).reshape(tokens, 3, local_inner)
    query = projected[:, 0].reshape(tokens, local_heads, HEAD_SIZE)
    key_value = projected[:, 1:]
    factor = HEAD_SIZE ** (-0.5)
    piece = lax.all_gather(key_value, "band", axis=0, tiled=True)
    running = jnp.full((local_heads, tokens), -1e30, jnp.float32)
    keys = piece[:, 0].reshape(piece.shape[0], local_heads, HEAD_SIZE)
    values = piece[:, 1].reshape(piece.shape[0], local_heads, HEAD_SIZE)
    scores = jnp.einsum("qhd,khd->hqk", query, keys, preferred_element_type=jnp.float32) * factor
    highest = jnp.maximum(running, jnp.max(scores, axis=2))
    weights = jnp.exp(scores - highest[:, :, None])
    total = jnp.sum(weights, axis=2)
    summed_values = jnp.einsum(
        "hqk,khd->hqd", weights.astype(jnp.bfloat16), values, preferred_element_type=jnp.float32
    )
    running, total, summed_values = (highest, total, summed_values)
    attention = (
        jnp.transpose(summed_values / total[:, :, None], (1, 0, 2))
        .reshape(tokens, local_inner)
        .astype(jnp.bfloat16)
    )
    outgoing = contract_last(lax.all_gather(attention, "head", axis=1, tiled=True), output_weight)
    attended = (
        convolved.astype(jnp.float32) + output_bias + outgoing.reshape(band_rows, width, outputs)
    )
    return (convolved, attended.astype(jnp.bfloat16))


def pair_kernel(
    shape,
    lat_ref,
    prm_ref,
    kw_hbm,
    pj_hbm,
    ow_hbm,
    wide_ref,
    gain_ref,
    kw,
    pw,
    ow,
    stat_a,
    stat_b,
    grid_in,
    norm_in,
    qkv_out,
    qkv_in,
    att_out,
    att_in,
    conv_ref,
    local_sem,
    send_sem,
    recv_sem,
):
    parts, bands, heads, rows, local, width = shape
    channels = local * heads
    tokens = rows * width
    groups_here = local // (CHANNELS // NORM_GROUPS)
    group_width = local // groups_here
    g, b, h = lax.axis_index("groups"), lax.axis_index("band"), lax.axis_index("head")
    sibling = h + 1 - 2 * lax.rem(h, 2)
    cross = lax.rem(h + 2, heads)
    far = lax.rem(sibling + 2, heads)
    used = [0]

    def remote(src, dst, groups=None, band=None, head=None):
        index = used[0]
        used[0] += 1
        return pltpu.make_async_remote_copy(
            src_ref=src,
            dst_ref=dst,
            send_sem=send_sem.at[index],
            recv_sem=recv_sem.at[index],
            device_id=(
                g if groups is None else groups,
                b if band is None else band,
                h if head is None else head,
            ),
            device_id_type=pl.DeviceIdType.MESH,
        )

    opened = []

    def begin(copy, sends=None):
        opened.append((copy, sends))
        if sends is None:
            copy.start()
        else:

            @pl.when(sends)
            def _():
                copy.start()

    def channel_rows(shard):
        return pl.ds(pl.multiple_of(shard * local, local), local)

    band_peers = [lax.rem(b + step, bands) for step in range(1, bands)]
    band_sources = [lax.rem(b - step + bands, bands) for step in range(1, bands)]
    part_peers = [lax.rem(g + step, parts) for step in range(1, parts)]
    part_sources = [lax.rem(g - step + parts, parts) for step in range(1, parts)]

    load_kernel = pltpu.make_async_copy(kw_hbm, kw, local_sem.at[0])
    load_output = pltpu.make_async_copy(ow_hbm, ow, local_sem.at[1])
    load_rows = pltpu.make_async_copy(pj_hbm, pw.at[:, channel_rows(b), :], local_sem.at[2])
    load_kernel.start()
    load_output.start()
    load_rows.start()

    barrier = pltpu.get_barrier_semaphore()
    neighbours = (
        [(g, b, sibling), (g, b, cross)]
        + [(g, peer, h) for peer in band_peers]
        + [(peer, b, h) for peer in part_peers]
    )
    for neighbour in neighbours:
        pl.semaphore_signal(
            barrier, inc=1, device_id=neighbour, device_id_type=pl.DeviceIdType.MESH
        )

    def statistics(read, stat):
        values = [
            read(row).astype(jnp.float32).reshape(groups_here, group_width, width)
            for row in range(rows)
        ]
        count = rows * width * group_width
        total = sum(jnp.sum(value, axis=1) for value in values)
        mean = jnp.sum(total, axis=1, keepdims=True) / count
        mean = jnp.broadcast_to(mean, (groups_here, width))
        squares = 0.0
        for value in values:
            centered = value - mean[:, None, :]
            squares = squares + jnp.sum(centered * centered, axis=1)
        squares = jnp.sum(squares, axis=1, keepdims=True)
        stat[b, 0] = mean
        stat[b, 1] = jnp.broadcast_to(squares, (groups_here, width))

    def exchange(stat):
        return [remote(stat.at[b], stat.at[b], band=peer) for peer in band_peers]

    def combined(stat):
        count = rows * width * group_width
        means = [stat[index, 0] for index in range(bands)]
        mean = sum(means) / bands
        spread = 0.0
        for index in range(bands):
            offset = means[index] - mean
            spread = spread + (stat[index, 1] + offset * offset * count)
        return mean, lax.rsqrt(spread / (count * bands) + 1e-05)

    def normalized(value, mean, scale, gain, shift):
        grouped = value.astype(jnp.float32).reshape(groups_here, group_width, width)
        scaled = (grouped - mean[:, None, :]) * scale[:, None, :]
        return scaled.reshape(local, width) * gain + shift

    params = prm_ref[...]
    lanes = params.shape[1]
    padded = jnp.concatenate(
        [params, jnp.zeros((lanes - params.shape[0], lanes), jnp.float32)], axis=0
    )
    columns = padded.T
    blocks = -(-local // lanes)

    def column(index):
        pieces = [columns[:, index * blocks + k : index * blocks + k + 1] for k in range(blocks)]
        return jnp.concatenate(pieces, axis=0)[:local]

    statistics(lambda row: lat_ref[row], stat_a)
    pl.semaphore_wait(barrier, len(neighbours))
    first = exchange(stat_a)
    for copy in first:
        begin(copy)

    share = local // parts

    def share_rows(band, part):
        return pl.ds(pl.multiple_of(band * local + part * share, share), share)

    weights = [
        remote(
            pj_hbm.at[:, pl.ds(pl.multiple_of(g * share, share), share), :],
            pw.at[:, share_rows(b, g), :],
            band=peer,
        )
        for peer in band_peers
    ]
    order = sorted(range(bands - 1), key=lambda index: index % 2)
    passed = []

    def pass_rows(index):
        weights[index].wait_recv()
        onward = pw.at[:, share_rows(band_sources[index], g), :]
        for peer in part_peers:
            move = remote(onward, onward, groups=peer)
            begin(move)
            passed.append(move)

    begin(weights[order[0]])
    for copy in first:
        copy.wait_recv()

    mean, scale = combined(stat_a)
    mine, crossed, sibs, fars = (channel_rows(s) for s in (h, cross, sibling, far))
    for row in range(rows):
        value = normalized(lat_ref[row], mean, scale, column(0), column(1))
        grid_in[row + 1, mine, :] = (value / (1.0 + jnp.exp(-value))).astype(jnp.bfloat16)

    def gather_pieces(buffer, pieces):
        sent = []
        for piece in pieces:
            own = buffer.at[piece, mine, :]
            there = buffer.at[piece, crossed, :]
            sent.append(
                (
                    remote(own, own, head=cross),
                    remote(own, own, head=sibling),
                    remote(there, there, head=sibling),
                )
            )
        return sent

    edges = (pl.ds(rows, 1), pl.ds(1, 1), pl.ds(2, rows - 2))
    gathered = gather_pieces(grid_in, edges)
    below, above = lax.rem(b + 1, bands), lax.rem(b + bands - 1, bands)
    halo = []
    for source, target, peer, sends, receives in (
        (rows, 0, below, b < bands - 1, b > 0),
        (1, rows + 1, above, b > 0, b < bands - 1),
    ):
        for shard in (mine, crossed):
            move = remote(grid_in.at[source, shard, :], grid_in.at[target, shard, :], band=peer)
            onward = grid_in.at[target, shard, :]
            halo.append((move, remote(onward, onward, head=sibling), sends, receives))
    for to_cross, to_sibling, _ in gathered:
        begin(to_cross)
        begin(to_sibling)
    for index in (0, 2):
        move, _, sends, _ = halo[index]
        begin(move, sends)

    pass_rows(order[0])
    for index in order[1:2]:
        begin(weights[index])
    for index, (to_cross, _, onward) in enumerate(gathered):
        to_cross.wait_recv()
        begin(onward)
        if index < 2:
            move, _, sends, _ = halo[2 * index + 1]
            begin(move, sends)

    for index in order[2:]:
        begin(weights[index])
    for target, receives in ((0, b > 0), (rows + 1, b < bands - 1)):

        @pl.when(jnp.logical_not(receives))
        def _(target=target):
            grid_in[target] = jnp.zeros((channels, width), jnp.bfloat16)

    for move, onward, _, receives in halo:

        @pl.when(receives)
        def _(move=move):
            move.wait_recv()

        begin(onward, receives)

    for _, to_sibling, onward in gathered:
        to_sibling.wait_recv()
        onward.wait_recv()
    for _, onward, _, receives in halo:

        @pl.when(receives)
        def _(onward=onward):
            onward.wait_recv()

    for index in order[1:2]:
        pass_rows(index)
    load_kernel.wait()
    taps = []
    for beside in range(3):
        summed = None
        for over in range(3):
            window = jnp.concatenate([grid_in[over + row] for row in range(rows)], axis=1)
            part = jnp.dot(kw[over, beside], window, preferred_element_type=jnp.float32)
            summed = part if summed is None else summed + part
        taps.append(summed)
    place = lax.broadcasted_iota(jnp.int32, (local, width), 1)
    bias = column(2)
    for row in range(rows):
        span = slice(row * width, (row + 1) * width)
        left = jnp.where(place == 0, 0.0, pltpu.roll(taps[0][:, span], 1, 1))
        right = jnp.where(place == width - 1, 0.0, pltpu.roll(taps[2][:, span], width - 1, 1))
        value = lat_ref[row].astype(jnp.float32) + bias + (taps[1][:, span] + left + right)
        wide_ref[row] = value
        conv_ref[row] = value.astype(jnp.bfloat16)

    statistics(lambda row: conv_ref[row], stat_b)
    second = exchange(stat_b)
    for copy in second:
        begin(copy)

    for copy in second:
        copy.wait_recv()
    mean, scale = combined(stat_b)
    for row in range(rows):
        value = normalized(conv_ref[row], mean, scale, column(3), column(4))
        norm_in[row, mine, :] = value.astype(jnp.bfloat16)
    normed = gather_pieces(norm_in, (pl.ds(0, rows),))
    for to_cross, to_sibling, onward in normed:
        begin(to_cross)
        begin(to_sibling)
    for index in order[2:]:
        pass_rows(index)
    for to_cross, _, onward in normed:
        to_cross.wait_recv()
        begin(onward)
    load_rows.wait()
    for move in passed:
        move.wait_recv()
    for to_cross, to_sibling, onward in normed:
        to_sibling.wait_recv()
        onward.wait_recv()

    features = jnp.concatenate([norm_in[row] for row in range(rows)], axis=1)
    contract_first = lambda left, right: lax.dot_general(
        left, right, (((0,), (0,)), ((), ())), preferred_element_type=jnp.float32
    )
    spread = []
    for kind in range(3):
        made = contract_first(pw[kind], features).astype(jnp.bfloat16)
        for head in range(bands):
            qkv_out[head, kind] = made[head * HEAD_SIZE : (head + 1) * HEAD_SIZE]
        qkv_in[b, kind] = qkv_out[b, kind]
        moves = [
            remote(qkv_out.at[peer, kind], qkv_in.at[b, kind], band=peer) for peer in band_peers
        ]
        for copy in moves:
            begin(copy)
        spread.append(moves)

    inner = bands * HEAD_SIZE
    factor = HEAD_SIZE ** (-0.5) * math.log2(math.e)

    def feature_rows(shard, band):
        return pl.ds(pl.multiple_of(shard * inner + band * HEAD_SIZE, HEAD_SIZE), HEAD_SIZE)

    onwards = [lax.rem(b + step, bands) for step in range(bands)]
    returned = [
        remote(att_out.at[index], att_in.at[feature_rows(h, b), :], band=source)
        for index, source in enumerate(band_sources)
    ]
    final = []
    for source in onwards:
        own = att_in.at[feature_rows(h, source), :]
        there = att_in.at[feature_rows(cross, source), :]
        final.append(
            (
                remote(own, own, head=cross),
                remote(own, own, head=sibling),
                remote(there, there, head=sibling),
            )
        )

    def pass_on(index):
        if index > 0:
            returned[index - 1].wait_recv()
        begin(final[index][0])
        begin(final[index][1])

    def relay(index):
        final[index][0].wait_recv()
        begin(final[index][2])

    for moves in spread:
        for copy in moves:
            copy.wait_recv()
    keys = jnp.concatenate([qkv_in[source, 1] for source in range(bands)], axis=1).T
    values = jnp.concatenate([qkv_in[source, 2] for source in range(bands)], axis=1)
    for index in list(range(1, bands)) + [0]:
        query = qkv_in[b if index == 0 else band_sources[index - 1], 0]
        scores = jnp.dot(keys, query, preferred_element_type=jnp.float32)
        top = jnp.max(scores, axis=0, keepdims=True)
        heavy = jnp.exp2((scores - top) * factor)
        total = jnp.sum(heavy, axis=0, keepdims=True)
        mixed = jnp.dot(values, heavy.astype(jnp.bfloat16), preferred_element_type=jnp.float32)
        result = (mixed / total).astype(jnp.bfloat16)
        if index > 0:
            att_out[index - 1] = result
            begin(returned[index - 1])
            if index > 1:
                pass_on(index - 1)
            if index > 2:
                relay(index - 2)
        else:
            att_in[feature_rows(h, b), :] = result
            pass_on(0)
    pass_on(bands - 1)
    for index in list(range(max(bands - 2, 1), bands)) + [0]:
        relay(index)
    load_output.wait()
    for _, to_sibling, onward in final:
        to_sibling.wait_recv()
        onward.wait_recv()
    outgoing = jnp.dot(ow[...], att_in[...], preferred_element_type=jnp.float32)
    bias = column(5)
    for row in range(rows):
        span = slice(row * width, (row + 1) * width)
        gain_ref[row] = outgoing[:, span] + bias

    for copy, sends in opened:
        if sends is None:
            copy.wait_send()
        else:

            @pl.when(sends)
            def _(copy=copy):
                copy.wait_send()


def pair_shards(
    parts,
    bands,
    heads,
    latent,
    first_gain,
    first_shift,
    kernel,
    kernel_bias,
    second_gain,
    second_shift,
    projection,
    output_weight,
    output_bias,
):
    rows, width, local = latent.shape
    channels, tokens = local * heads, rows * width
    inner = projection.shape[2]
    groups_here = local // (CHANNELS // NORM_GROUPS)
    vectors = [first_gain, first_shift, kernel_bias, second_gain, second_shift, output_bias]
    gap = jnp.zeros((-local % 128,), jnp.float32)
    flat = jnp.concatenate([piece for vector in vectors for piece in (vector, gap)])
    params = jnp.pad(flat, (0, -flat.shape[0] % 1024)).reshape(-1, 128)
    vmem = pl.BlockSpec(memory_space=pltpu.VMEM)
    hbm = pl.BlockSpec(memory_space=pl.ANY)
    result = jax.ShapeDtypeStruct((rows, local, width), jnp.float32)
    copies = 64
    call = pl.pallas_call(
        functools.partial(pair_kernel, (parts, bands, heads, rows, local, width)),
        out_shape=(result, result),
        in_specs=[vmem, vmem, hbm, hbm, hbm],
        out_specs=(vmem, vmem),
        scratch_shapes=[
            pltpu.VMEM((3, 3, local, channels), jnp.bfloat16),
            pltpu.VMEM((3, channels, inner), jnp.bfloat16),
            pltpu.VMEM((local, inner * heads), jnp.bfloat16),
            pltpu.VMEM((bands, 2, groups_here, width), jnp.float32),
            pltpu.VMEM((bands, 2, groups_here, width), jnp.float32),
            pltpu.VMEM((rows + 2, channels, width), jnp.bfloat16),
            pltpu.VMEM((rows, channels, width), jnp.bfloat16),
            pltpu.VMEM((bands, 3, HEAD_SIZE, tokens), jnp.bfloat16),
            pltpu.VMEM((bands, 3, HEAD_SIZE, tokens), jnp.bfloat16),
            pltpu.VMEM((bands - 1, HEAD_SIZE, tokens), jnp.bfloat16),
            pltpu.VMEM((inner * heads, tokens), jnp.bfloat16),
            pltpu.VMEM((rows, local, width), jnp.bfloat16),
            pltpu.SemaphoreType.DMA((3,)),
            pltpu.SemaphoreType.DMA((copies,)),
            pltpu.SemaphoreType.DMA((copies,)),
        ],
        compiler_params=pltpu.CompilerParams(
            collective_id=0, has_side_effects=True, vmem_limit_bytes=60 << 20
        ),
    )
    wide, gained = call(
        jnp.transpose(latent, (0, 2, 1)),
        params,
        jnp.transpose(kernel, (1, 2, 0, 3)),
        jnp.transpose(projection, (1, 0, 2)),
        output_weight,
    )
    convolved = jnp.transpose(wide, (0, 2, 1)).astype(jnp.bfloat16)
    attended = convolved.astype(jnp.float32) + jnp.transpose(gained, (0, 2, 1))
    return convolved, attended.astype(jnp.bfloat16)


def solution(mesh):
    placed = (
        P(("groups", "band"), None, "head"),
        P("head"),
        P("head"),
        P("head", None, None, None),
        P("head"),
        P("head"),
        P("head"),
        P("band", None, "head"),
        P("head", None),
        P("head"),
    )
    parts, bands, heads = (mesh.shape[axis] for axis in ("groups", "band", "head"))
    paired = heads == 4 and bands > 1 and HEADS == heads * bands and CHANNELS % (16 * parts * heads) == 0
    body = functools.partial(pair_shards, parts, bands, heads) if paired else shards
    return jax.shard_map(
        body,
        mesh=mesh,
        in_specs=placed,
        out_specs=(P(("groups", "band"), None, "head"), P(("groups", "band"), None, "head")),
        check_vma=False,
    )
```

```python
import functools
import math

import jax
import jax.numpy as jnp
from jax import lax
from jax.experimental import pallas as pl
from jax.experimental.pallas import tpu as pltpu
from jax.sharding import PartitionSpec as P

CHANNELS = 1280
HEADS = 16
HEAD_SIZE = 64
NORM_GROUPS = 32


def padded_2(cells, sides, width):
    for axis, dim in sides:
        count = lax.axis_size(axis)
        ends = count - 1
        head = lax.slice_in_dim(cells, 0, width, axis=dim)
        tail = lax.slice_in_dim(cells, cells.shape[dim] - width, cells.shape[dim], axis=dim)
        cells = jnp.concatenate(
            [
                lax.ppermute(tail, axis, [(i, (i + 1) % count) for i in range(ends)]),
                cells,
                lax.ppermute(head, axis, [((i + 1) % count, i) for i in range(ends)]),
            ],
            axis=dim,
        )
    return cells


def normalize(values, gain, shift, group_width, count):
    band_rows, width, channels = values.shape
    grouped = values.reshape(band_rows * width, channels // group_width, group_width)
    mean = lax.psum(jnp.sum(grouped, axis=(0, 2)), "band") / count
    centered = grouped - mean[None, :, None]
    spread = lax.psum(jnp.sum(centered * centered, axis=(0, 2)), "band") / count
    scaled = centered * lax.rsqrt(spread + 1e-05)[None, :, None]
    return scaled.reshape(band_rows, width, channels) * gain + shift


def contract_last(left, right):
    return lax.dot_general(
        left, right, (((1,), (1,)), ((), ())), preferred_element_type=jnp.float32
    )


def kernel_block(padded, weights, band_rows, width):
    inputs = padded.shape[2]
    wide = jnp.pad(padded, ((0, 0), (1, 1), (0, 0)))
    summed = jnp.zeros((band_rows * width, weights.shape[0]), jnp.float32)
    for above in range(3):
        for beside in range(3):
            window = wide[above : above + band_rows, beside : beside + width, :].reshape(
                band_rows * width, inputs
            )
            summed = summed + contract_last(window, weights[:, above, beside, :])
    return summed


def shards(
    latent,
    first_gain,
    first_shift,
    kernel,
    kernel_bias,
    second_gain,
    second_shift,
    projection,
    output_weight,
    output_bias,
):
    band_rows, width, channels = latent.shape
    tokens = band_rows * width
    group_width = CHANNELS // NORM_GROUPS
    count = lax.axis_size("band") * band_rows * width * group_width
    outputs = kernel.shape[0]
    latent_wide = latent.astype(jnp.float32)
    activated = jax.nn.silu(
        normalize(latent_wide, first_gain, first_shift, group_width, count)
    ).astype(jnp.bfloat16)
    gathered = lax.all_gather(activated, "head", axis=2, tiled=True)
    padded = padded_2(gathered, (("band", 0),), 1)
    summed = kernel_block(padded, kernel, band_rows, width)
    convolved = (latent_wide + kernel_bias + summed.reshape(band_rows, width, outputs)).astype(
        jnp.bfloat16
    )
    normed = normalize(
        convolved.astype(jnp.float32), second_gain, second_shift, group_width, count
    ).astype(jnp.bfloat16)
    features = lax.all_gather(normed, "head", axis=2, tiled=True).reshape(tokens, CHANNELS)
    local_inner = projection.shape[2]
    local_heads = local_inner // HEAD_SIZE
    piece = lax.all_gather(projection, "band", axis=0, tiled=True)
    projected = jnp.dot(
        features, piece.reshape(piece.shape[0], 3 * local_inner), preferred_element_type=jnp.float32
    )
    projected = projected.astype(jnp.bfloat16).reshape(tokens, 3, local_inner)
    query = projected[:, 0].reshape(tokens, local_heads, HEAD_SIZE)
    key_value = projected[:, 1:]
    factor = HEAD_SIZE ** (-0.5)
    piece = lax.all_gather(key_value, "band", axis=0, tiled=True)
    running = jnp.full((local_heads, tokens), -1e30, jnp.float32)
    keys = piece[:, 0].reshape(piece.shape[0], local_heads, HEAD_SIZE)
    values = piece[:, 1].reshape(piece.shape[0], local_heads, HEAD_SIZE)
    scores = jnp.einsum("qhd,khd->hqk", query, keys, preferred_element_type=jnp.float32) * factor
    highest = jnp.maximum(running, jnp.max(scores, axis=2))
    weights = jnp.exp(scores - highest[:, :, None])
    total = jnp.sum(weights, axis=2)
    summed_values = jnp.einsum(
        "hqk,khd->hqd", weights.astype(jnp.bfloat16), values, preferred_element_type=jnp.float32
    )
    running, total, summed_values = (highest, total, summed_values)
    attention = (
        jnp.transpose(summed_values / total[:, :, None], (1, 0, 2))
        .reshape(tokens, local_inner)
        .astype(jnp.bfloat16)
    )
    outgoing = contract_last(lax.all_gather(attention, "head", axis=1, tiled=True), output_weight)
    attended = (
        convolved.astype(jnp.float32) + output_bias + outgoing.reshape(band_rows, width, outputs)
    )
    return (convolved, attended.astype(jnp.bfloat16))


def pair_kernel(
    shape,
    lat_ref,
    prm_ref,
    kw_hbm,
    pj_hbm,
    ow_hbm,
    wide_ref,
    gain_ref,
    kw,
    pw,
    ow,
    stat_a,
    stat_b,
    grid_in,
    norm_in,
    qkv_out,
    qkv_in,
    att_out,
    att_in,
    conv_ref,
    local_sem,
    send_sem,
    recv_sem,
):
    parts, bands, heads, rows, local, width = shape
    channels = local * heads
    tokens = rows * width
    groups_here = local // (CHANNELS // NORM_GROUPS)
    group_width = local // groups_here
    g, b, h = lax.axis_index("groups"), lax.axis_index("band"), lax.axis_index("head")
    sibling = h + 1 - 2 * lax.rem(h, 2)
    cross = lax.rem(h + 2, heads)
    far = lax.rem(sibling + 2, heads)
    used = [0]

    def remote(src, dst, groups=None, band=None, head=None):
        index = used[0]
        used[0] += 1
        return pltpu.make_async_remote_copy(
            src_ref=src,
            dst_ref=dst,
            send_sem=send_sem.at[index],
            recv_sem=recv_sem.at[index],
            device_id=(
                g if groups is None else groups,
                b if band is None else band,
                h if head is None else head,
            ),
            device_id_type=pl.DeviceIdType.MESH,
        )

    opened = []

    def begin(copy, sends=None):
        opened.append((copy, sends))
        if sends is None:
            copy.start()
        else:

            @pl.when(sends)
            def _():
                copy.start()

    def channel_rows(shard):
        return pl.ds(pl.multiple_of(shard * local, local), local)

    band_peers = [lax.rem(b + step, bands) for step in range(1, bands)]
    band_sources = [lax.rem(b - step + bands, bands) for step in range(1, bands)]
    part_peers = [lax.rem(g + step, parts) for step in range(1, parts)]
    part_sources = [lax.rem(g - step + parts, parts) for step in range(1, parts)]

    load_kernel = pltpu.make_async_copy(kw_hbm, kw, local_sem.at[0])
    load_output = pltpu.make_async_copy(ow_hbm, ow, local_sem.at[1])
    load_rows = pltpu.make_async_copy(pj_hbm, pw.at[:, channel_rows(b), :], local_sem.at[2])
    load_kernel.start()
    load_output.start()
    load_rows.start()

    barrier = pltpu.get_barrier_semaphore()
    neighbours = (
        [(g, b, sibling), (g, b, cross)]
        + [(g, peer, h) for peer in band_peers]
        + [(peer, b, h) for peer in part_peers]
    )
    for neighbour in neighbours:
        pl.semaphore_signal(
            barrier, inc=1, device_id=neighbour, device_id_type=pl.DeviceIdType.MESH
        )

    def statistics(read, stat):
        values = [
            read(row).astype(jnp.float32).reshape(groups_here, group_width, width)
            for row in range(rows)
        ]
        count = rows * width * group_width
        total = sum(jnp.sum(value, axis=1) for value in values)
        mean = jnp.sum(total, axis=1, keepdims=True) / count
        mean = jnp.broadcast_to(mean, (groups_here, width))
        squares = 0.0
        for value in values:
            centered = value - mean[:, None, :]
            squares = squares + jnp.sum(centered * centered, axis=1)
        squares = jnp.sum(squares, axis=1, keepdims=True)
        stat[b, 0] = mean
        stat[b, 1] = jnp.broadcast_to(squares, (groups_here, width))

    def exchange(stat):
        return [remote(stat.at[b], stat.at[b], band=peer) for peer in band_peers]

    def combined(stat):
        count = rows * width * group_width
        means = [stat[index, 0] for index in range(bands)]
        mean = sum(means) / bands
        spread = 0.0
        for index in range(bands):
            offset = means[index] - mean
            spread = spread + (stat[index, 1] + offset * offset * count)
        return mean, lax.rsqrt(spread / (count * bands) + 1e-05)

    def normalized(value, mean, scale, gain, shift):
        grouped = value.astype(jnp.float32).reshape(groups_here, group_width, width)
        scaled = (grouped - mean[:, None, :]) * scale[:, None, :]
        return scaled.reshape(local, width) * gain + shift

    params = prm_ref[...]
    lanes = params.shape[1]
    padded = jnp.concatenate(
        [params, jnp.zeros((lanes - params.shape[0], lanes), jnp.float32)], axis=0
    )
    columns = padded.T
    blocks = -(-local // lanes)

    def column(index):
        pieces = [columns[:, index * blocks + k : index * blocks + k + 1] for k in range(blocks)]
        return jnp.concatenate(pieces, axis=0)[:local]

    statistics(lambda row: lat_ref[row], stat_a)
    pl.semaphore_wait(barrier, len(neighbours))
    first = exchange(stat_a)
    for copy in first:
        begin(copy)

    share = local // parts

    def share_rows(band, part):
        return pl.ds(pl.multiple_of(band * local + part * share, share), share)

    weights = [
        remote(
            pj_hbm.at[:, pl.ds(pl.multiple_of(g * share, share), share), :],
            pw.at[:, share_rows(b, g), :],
            band=peer,
        )
        for peer in band_peers
    ]
    order = sorted(range(bands - 1), key=lambda index: index % 2)
    passed = []

    def pass_rows(index):
        weights[index].wait_recv()
        onward = pw.at[:, share_rows(band_sources[index], g), :]
        for peer in part_peers:
            move = remote(onward, onward, groups=peer)
            begin(move)
            passed.append(move)

    begin(weights[order[0]])
    for copy in first:
        copy.wait_recv()

    mean, scale = combined(stat_a)
    mine, crossed, sibs, fars = (channel_rows(s) for s in (h, cross, sibling, far))
    for row in range(rows):
        value = normalized(lat_ref[row], mean, scale, column(0), column(1))
        grid_in[row + 1, mine, :] = (value / (1.0 + jnp.exp(-value))).astype(jnp.bfloat16)

    def gather_pieces(buffer, pieces):
        sent = []
        for piece in pieces:
            own = buffer.at[piece, mine, :]
            there = buffer.at[piece, crossed, :]
            sent.append(
                (
                    remote(own, own, head=cross),
                    remote(own, own, head=sibling),
                    remote(there, there, head=sibling),
                )
            )
        return sent

    edges = (pl.ds(rows, 1), pl.ds(1, 1), pl.ds(2, rows - 2))
    gathered = gather_pieces(grid_in, edges)
    below, above = lax.rem(b + 1, bands), lax.rem(b + bands - 1, bands)
    halo = []
    for source, target, peer, sends, receives in (
        (rows, 0, below, b < bands - 1, b > 0),
        (1, rows + 1, above, b > 0, b < bands - 1),
    ):
        for shard in (mine, crossed):
            move = remote(grid_in.at[source, shard, :], grid_in.at[target, shard, :], band=peer)
            onward = grid_in.at[target, shard, :]
            halo.append((move, remote(onward, onward, head=sibling), sends, receives))
    for to_cross, to_sibling, _ in gathered:
        begin(to_cross)
        begin(to_sibling)
    for index in (0, 2):
        move, _, sends, _ = halo[index]
        begin(move, sends)

    for index, (to_cross, _, onward) in enumerate(gathered):
        to_cross.wait_recv()
        begin(onward)
        if index < 2:
            move, _, sends, _ = halo[2 * index + 1]
            begin(move, sends)

    pass_rows(order[0])
    for index in order[1:]:
        begin(weights[index])
    for target, receives in ((0, b > 0), (rows + 1, b < bands - 1)):

        @pl.when(jnp.logical_not(receives))
        def _(target=target):
            grid_in[target] = jnp.zeros((channels, width), jnp.bfloat16)

    for move, onward, _, receives in halo:

        @pl.when(receives)
        def _(move=move):
            move.wait_recv()

        begin(onward, receives)

    for _, to_sibling, onward in gathered:
        to_sibling.wait_recv()
        onward.wait_recv()
    for _, onward, _, receives in halo:

        @pl.when(receives)
        def _(onward=onward):
            onward.wait_recv()

    load_kernel.wait()
    taps = []
    for beside in range(3):
        summed = None
        for over in range(3):
            window = jnp.concatenate([grid_in[over + row] for row in range(rows)], axis=1)
            part = jnp.dot(kw[over, beside], window, preferred_element_type=jnp.float32)
            summed = part if summed is None else summed + part
        taps.append(summed)
    place = lax.broadcasted_iota(jnp.int32, (local, width), 1)
    bias = column(2)
    for row in range(rows):
        span = slice(row * width, (row + 1) * width)
        left = jnp.where(place == 0, 0.0, pltpu.roll(taps[0][:, span], 1, 1))
        right = jnp.where(place == width - 1, 0.0, pltpu.roll(taps[2][:, span], width - 1, 1))
        value = lat_ref[row].astype(jnp.float32) + bias + (taps[1][:, span] + left + right)
        wide_ref[row] = value
        conv_ref[row] = value.astype(jnp.bfloat16)

    statistics(lambda row: conv_ref[row], stat_b)
    second = exchange(stat_b)
    for copy in second:
        begin(copy)
    for index in order[1:2]:
        pass_rows(index)

    for copy in second:
        copy.wait_recv()
    mean, scale = combined(stat_b)
    for row in range(rows):
        value = normalized(conv_ref[row], mean, scale, column(3), column(4))
        norm_in[row, mine, :] = value.astype(jnp.bfloat16)
    normed = gather_pieces(norm_in, (pl.ds(0, rows),))
    for to_cross, to_sibling, onward in normed:
        begin(to_cross)
        begin(to_sibling)
    for index in order[2:]:
        pass_rows(index)
    for to_cross, _, onward in normed:
        to_cross.wait_recv()
        begin(onward)
    load_rows.wait()
    for move in passed:
        move.wait_recv()
    for to_cross, to_sibling, onward in normed:
        to_sibling.wait_recv()
        onward.wait_recv()

    features = jnp.concatenate([norm_in[row] for row in range(rows)], axis=1)
    contract_first = lambda left, right: lax.dot_general(
        left, right, (((0,), (0,)), ((), ())), preferred_element_type=jnp.float32
    )
    spread = []
    for kind in range(3):
        made = contract_first(pw[kind], features).astype(jnp.bfloat16)
        for head in range(bands):
            qkv_out[head, kind] = made[head * HEAD_SIZE : (head + 1) * HEAD_SIZE]
        qkv_in[b, kind] = qkv_out[b, kind]
        moves = [
            remote(qkv_out.at[peer, kind], qkv_in.at[b, kind], band=peer) for peer in band_peers
        ]
        for copy in moves:
            begin(copy)
        spread.append(moves)

    inner = bands * HEAD_SIZE
    factor = HEAD_SIZE ** (-0.5) * math.log2(math.e)

    def feature_rows(shard, band):
        return pl.ds(pl.multiple_of(shard * inner + band * HEAD_SIZE, HEAD_SIZE), HEAD_SIZE)

    onwards = [lax.rem(b + step, bands) for step in range(bands)]
    returned = [
        remote(att_out.at[index], att_in.at[feature_rows(h, b), :], band=source)
        for index, source in enumerate(band_sources)
    ]
    final = []
    for source in onwards:
        own = att_in.at[feature_rows(h, source), :]
        there = att_in.at[feature_rows(cross, source), :]
        final.append(
            (
                remote(own, own, head=cross),
                remote(own, own, head=sibling),
                remote(there, there, head=sibling),
            )
        )

    def pass_on(index):
        if index > 0:
            returned[index - 1].wait_recv()
        begin(final[index][0])
        begin(final[index][1])

    def relay(index):
        final[index][0].wait_recv()
        begin(final[index][2])

    for moves in spread[:2]:
        for copy in moves:
            copy.wait_recv()
    keys = jnp.concatenate([qkv_in[source, 1] for source in range(bands)], axis=1).T
    values = None
    for index in list(range(1, bands)) + [0]:
        query = qkv_in[b if index == 0 else band_sources[index - 1], 0]
        scores = jnp.dot(keys, query, preferred_element_type=jnp.float32)
        top = jnp.max(scores, axis=0, keepdims=True)
        heavy = jnp.exp2((scores - top) * factor)
        total = jnp.sum(heavy, axis=0, keepdims=True)
        if values is None:
            for copy in spread[2]:
                copy.wait_recv()
            values = jnp.concatenate([qkv_in[source, 2] for source in range(bands)], axis=1)
        mixed = jnp.dot(values, heavy.astype(jnp.bfloat16), preferred_element_type=jnp.float32)
        result = (mixed / total).astype(jnp.bfloat16)
        if index > 0:
            att_out[index - 1] = result
            begin(returned[index - 1])
            if index > 1:
                pass_on(index - 1)
            if index > 2:
                relay(index - 2)
        else:
            att_in[feature_rows(h, b), :] = result
            pass_on(0)
    pass_on(bands - 1)
    for index in list(range(max(bands - 2, 1), bands)) + [0]:
        relay(index)
    load_output.wait()
    for _, to_sibling, onward in final:
        to_sibling.wait_recv()
        onward.wait_recv()
    outgoing = jnp.dot(ow[...], att_in[...], preferred_element_type=jnp.float32)
    bias = column(5)
    for row in range(rows):
        span = slice(row * width, (row + 1) * width)
        gain_ref[row] = conv_ref[row].astype(jnp.float32) + bias + outgoing[:, span]

    for copy, sends in opened:
        if sends is None:
            copy.wait_send()
        else:

            @pl.when(sends)
            def _(copy=copy):
                copy.wait_send()


def pair_shards(
    parts,
    bands,
    heads,
    latent,
    first_gain,
    first_shift,
    kernel,
    kernel_bias,
    second_gain,
    second_shift,
    projection,
    output_weight,
    output_bias,
):
    rows, width, local = latent.shape
    channels, tokens = local * heads, rows * width
    inner = projection.shape[2]
    groups_here = local // (CHANNELS // NORM_GROUPS)
    vectors = [first_gain, first_shift, kernel_bias, second_gain, second_shift, output_bias]
    gap = jnp.zeros((-local % 128,), jnp.float32)
    flat = jnp.concatenate([piece for vector in vectors for piece in (vector, gap)])
    params = jnp.pad(flat, (0, -flat.shape[0] % 1024)).reshape(-1, 128)
    vmem = pl.BlockSpec(memory_space=pltpu.VMEM)
    hbm = pl.BlockSpec(memory_space=pl.ANY)
    result = jax.ShapeDtypeStruct((rows, local, width), jnp.float32)
    copies = 64
    call = pl.pallas_call(
        functools.partial(pair_kernel, (parts, bands, heads, rows, local, width)),
        out_shape=(result, result),
        in_specs=[vmem, vmem, hbm, hbm, hbm],
        out_specs=(vmem, vmem),
        scratch_shapes=[
            pltpu.VMEM((3, 3, local, channels), jnp.bfloat16),
            pltpu.VMEM((3, channels, inner), jnp.bfloat16),
            pltpu.VMEM((local, inner * heads), jnp.bfloat16),
            pltpu.VMEM((bands, 2, groups_here, width), jnp.float32),
            pltpu.VMEM((bands, 2, groups_here, width), jnp.float32),
            pltpu.VMEM((rows + 2, channels, width), jnp.bfloat16),
            pltpu.VMEM((rows, channels, width), jnp.bfloat16),
            pltpu.VMEM((bands, 3, HEAD_SIZE, tokens), jnp.bfloat16),
            pltpu.VMEM((bands, 3, HEAD_SIZE, tokens), jnp.bfloat16),
            pltpu.VMEM((bands - 1, HEAD_SIZE, tokens), jnp.bfloat16),
            pltpu.VMEM((inner * heads, tokens), jnp.bfloat16),
            pltpu.VMEM((rows, local, width), jnp.bfloat16),
            pltpu.SemaphoreType.DMA((3,)),
            pltpu.SemaphoreType.DMA((copies,)),
            pltpu.SemaphoreType.DMA((copies,)),
        ],
        compiler_params=pltpu.CompilerParams(
            collective_id=0, has_side_effects=True, vmem_limit_bytes=60 << 20
        ),
    )
    wide, gained = call(
        jnp.transpose(latent, (0, 2, 1)),
        params,
        jnp.transpose(kernel, (1, 2, 0, 3)),
        jnp.transpose(projection, (1, 0, 2)),
        output_weight,
    )
    convolved = jnp.transpose(wide, (0, 2, 1)).astype(jnp.bfloat16)
    return convolved, jnp.transpose(gained, (0, 2, 1)).astype(jnp.bfloat16)


def solution(mesh):
    placed = (
        P(("groups", "band"), None, "head"),
        P("head"),
        P("head"),
        P("head", None, None, None),
        P("head"),
        P("head"),
        P("head"),
        P("band", None, "head"),
        P("head", None),
        P("head"),
    )
    parts, bands, heads = (mesh.shape[axis] for axis in ("groups", "band", "head"))
    paired = heads == 4 and bands > 1 and HEADS == heads * bands and CHANNELS % (16 * parts * heads) == 0
    body = functools.partial(pair_shards, parts, bands, heads) if paired else shards
    return jax.shard_map(
        body,
        mesh=mesh,
        in_specs=placed,
        out_specs=(P(("groups", "band"), None, "head"), P(("groups", "band"), None, "head")),
        check_vma=False,
    )
```

```python
import functools
import math

import jax
import jax.numpy as jnp
from jax import lax
from jax.experimental import pallas as pl
from jax.experimental.pallas import tpu as pltpu
from jax.sharding import PartitionSpec as P

CHANNELS = 1280
HEADS = 16
HEAD_SIZE = 64
NORM_GROUPS = 32


def padded_2(cells, sides, width):
    for axis, dim in sides:
        count = lax.axis_size(axis)
        ends = count - 1
        head = lax.slice_in_dim(cells, 0, width, axis=dim)
        tail = lax.slice_in_dim(cells, cells.shape[dim] - width, cells.shape[dim], axis=dim)
        cells = jnp.concatenate(
            [
                lax.ppermute(tail, axis, [(i, (i + 1) % count) for i in range(ends)]),
                cells,
                lax.ppermute(head, axis, [((i + 1) % count, i) for i in range(ends)]),
            ],
            axis=dim,
        )
    return cells


def normalize(values, gain, shift, group_width, count):
    band_rows, width, channels = values.shape
    grouped = values.reshape(band_rows * width, channels // group_width, group_width)
    mean = lax.psum(jnp.sum(grouped, axis=(0, 2)), "band") / count
    centered = grouped - mean[None, :, None]
    spread = lax.psum(jnp.sum(centered * centered, axis=(0, 2)), "band") / count
    scaled = centered * lax.rsqrt(spread + 1e-05)[None, :, None]
    return scaled.reshape(band_rows, width, channels) * gain + shift


def contract_last(left, right):
    return lax.dot_general(
        left, right, (((1,), (1,)), ((), ())), preferred_element_type=jnp.float32
    )


def kernel_block(padded, weights, band_rows, width):
    inputs = padded.shape[2]
    wide = jnp.pad(padded, ((0, 0), (1, 1), (0, 0)))
    summed = jnp.zeros((band_rows * width, weights.shape[0]), jnp.float32)
    for above in range(3):
        for beside in range(3):
            window = wide[above : above + band_rows, beside : beside + width, :].reshape(
                band_rows * width, inputs
            )
            summed = summed + contract_last(window, weights[:, above, beside, :])
    return summed


def shards(
    latent,
    first_gain,
    first_shift,
    kernel,
    kernel_bias,
    second_gain,
    second_shift,
    projection,
    output_weight,
    output_bias,
):
    band_rows, width, channels = latent.shape
    tokens = band_rows * width
    group_width = CHANNELS // NORM_GROUPS
    count = lax.axis_size("band") * band_rows * width * group_width
    outputs = kernel.shape[0]
    latent_wide = latent.astype(jnp.float32)
    activated = jax.nn.silu(
        normalize(latent_wide, first_gain, first_shift, group_width, count)
    ).astype(jnp.bfloat16)
    gathered = lax.all_gather(activated, "head", axis=2, tiled=True)
    padded = padded_2(gathered, (("band", 0),), 1)
    summed = kernel_block(padded, kernel, band_rows, width)
    convolved = (latent_wide + kernel_bias + summed.reshape(band_rows, width, outputs)).astype(
        jnp.bfloat16
    )
    normed = normalize(
        convolved.astype(jnp.float32), second_gain, second_shift, group_width, count
    ).astype(jnp.bfloat16)
    features = lax.all_gather(normed, "head", axis=2, tiled=True).reshape(tokens, CHANNELS)
    local_inner = projection.shape[2]
    local_heads = local_inner // HEAD_SIZE
    piece = lax.all_gather(projection, "band", axis=0, tiled=True)
    projected = jnp.dot(
        features, piece.reshape(piece.shape[0], 3 * local_inner), preferred_element_type=jnp.float32
    )
    projected = projected.astype(jnp.bfloat16).reshape(tokens, 3, local_inner)
    query = projected[:, 0].reshape(tokens, local_heads, HEAD_SIZE)
    key_value = projected[:, 1:]
    factor = HEAD_SIZE ** (-0.5)
    piece = lax.all_gather(key_value, "band", axis=0, tiled=True)
    running = jnp.full((local_heads, tokens), -1e30, jnp.float32)
    keys = piece[:, 0].reshape(piece.shape[0], local_heads, HEAD_SIZE)
    values = piece[:, 1].reshape(piece.shape[0], local_heads, HEAD_SIZE)
    scores = jnp.einsum("qhd,khd->hqk", query, keys, preferred_element_type=jnp.float32) * factor
    highest = jnp.maximum(running, jnp.max(scores, axis=2))
    weights = jnp.exp(scores - highest[:, :, None])
    total = jnp.sum(weights, axis=2)
    summed_values = jnp.einsum(
        "hqk,khd->hqd", weights.astype(jnp.bfloat16), values, preferred_element_type=jnp.float32
    )
    running, total, summed_values = (highest, total, summed_values)
    attention = (
        jnp.transpose(summed_values / total[:, :, None], (1, 0, 2))
        .reshape(tokens, local_inner)
        .astype(jnp.bfloat16)
    )
    outgoing = contract_last(lax.all_gather(attention, "head", axis=1, tiled=True), output_weight)
    attended = (
        convolved.astype(jnp.float32) + output_bias + outgoing.reshape(band_rows, width, outputs)
    )
    return (convolved, attended.astype(jnp.bfloat16))


def pair_kernel(
    shape,
    lat_ref,
    prm_ref,
    kw_hbm,
    pj_hbm,
    ow_hbm,
    wide_ref,
    gain_ref,
    kw,
    pw,
    ow,
    stat_a,
    stat_b,
    grid_in,
    norm_in,
    qkv_out,
    qkv_in,
    att_out,
    att_in,
    conv_ref,
    local_sem,
    send_sem,
    recv_sem,
):
    parts, bands, heads, rows, local, width = shape
    channels = local * heads
    tokens = rows * width
    groups_here = local // (CHANNELS // NORM_GROUPS)
    group_width = local // groups_here
    g, b, h = lax.axis_index("groups"), lax.axis_index("band"), lax.axis_index("head")
    sibling = h + 1 - 2 * lax.rem(h, 2)
    cross = lax.rem(h + 2, heads)
    far = lax.rem(sibling + 2, heads)
    used = [0]

    def remote(src, dst, groups=None, band=None, head=None):
        index = used[0]
        used[0] += 1
        return pltpu.make_async_remote_copy(
            src_ref=src,
            dst_ref=dst,
            send_sem=send_sem.at[index],
            recv_sem=recv_sem.at[index],
            device_id=(
                g if groups is None else groups,
                b if band is None else band,
                h if head is None else head,
            ),
            device_id_type=pl.DeviceIdType.MESH,
        )

    opened = []

    def begin(copy, sends=None):
        opened.append((copy, sends))
        if sends is None:
            copy.start()
        else:

            @pl.when(sends)
            def _():
                copy.start()

    def channel_rows(shard):
        return pl.ds(pl.multiple_of(shard * local, local), local)

    band_peers = [lax.rem(b + step, bands) for step in range(1, bands)]
    band_sources = [lax.rem(b - step + bands, bands) for step in range(1, bands)]
    part_peers = [lax.rem(g + step, parts) for step in range(1, parts)]
    part_sources = [lax.rem(g - step + parts, parts) for step in range(1, parts)]

    load_kernel = pltpu.make_async_copy(kw_hbm, kw, local_sem.at[0])
    load_output = pltpu.make_async_copy(ow_hbm, ow, local_sem.at[1])
    load_rows = pltpu.make_async_copy(pj_hbm, pw.at[:, channel_rows(b), :], local_sem.at[2])
    load_kernel.start()
    load_output.start()
    load_rows.start()

    barrier = pltpu.get_barrier_semaphore()
    neighbours = (
        [(g, b, sibling), (g, b, cross)]
        + [(g, peer, h) for peer in band_peers]
        + [(peer, b, h) for peer in part_peers]
    )
    for neighbour in neighbours:
        pl.semaphore_signal(
            barrier, inc=1, device_id=neighbour, device_id_type=pl.DeviceIdType.MESH
        )

    def statistics(read, stat):
        values = [
            read(row).astype(jnp.float32).reshape(groups_here, group_width, width)
            for row in range(rows)
        ]
        count = rows * width * group_width
        total = sum(jnp.sum(value, axis=1) for value in values)
        mean = jnp.sum(total, axis=1, keepdims=True) / count
        mean = jnp.broadcast_to(mean, (groups_here, width))
        squares = 0.0
        for value in values:
            centered = value - mean[:, None, :]
            squares = squares + jnp.sum(centered * centered, axis=1)
        squares = jnp.sum(squares, axis=1, keepdims=True)
        stat[b, 0] = mean
        stat[b, 1] = jnp.broadcast_to(squares, (groups_here, width))

    def exchange(stat):
        return [remote(stat.at[b], stat.at[b], band=peer) for peer in band_peers]

    def combined(stat):
        count = rows * width * group_width
        means = [stat[index, 0] for index in range(bands)]
        mean = sum(means) / bands
        spread = 0.0
        for index in range(bands):
            offset = means[index] - mean
            spread = spread + (stat[index, 1] + offset * offset * count)
        return mean, lax.rsqrt(spread / (count * bands) + 1e-05)

    def normalized(value, mean, scale, gain, shift):
        grouped = value.astype(jnp.float32).reshape(groups_here, group_width, width)
        scaled = (grouped - mean[:, None, :]) * scale[:, None, :]
        return scaled.reshape(local, width) * gain + shift

    params = prm_ref[...]
    lanes = params.shape[1]
    padded = jnp.concatenate(
        [params, jnp.zeros((lanes - params.shape[0], lanes), jnp.float32)], axis=0
    )
    columns = padded.T
    blocks = -(-local // lanes)

    def column(index):
        pieces = [columns[:, index * blocks + k : index * blocks + k + 1] for k in range(blocks)]
        return jnp.concatenate(pieces, axis=0)[:local]

    statistics(lambda row: lat_ref[row], stat_a)
    pl.semaphore_wait(barrier, len(neighbours))
    first = exchange(stat_a)
    for copy in first:
        begin(copy)

    share = local // parts

    def share_rows(band, part):
        return pl.ds(pl.multiple_of(band * local + part * share, share), share)

    passed = []
    hops = []
    for hop in range(1, bands):
        pair = []
        for sign, peer in ((1, lax.rem(b + 1, bands)), (-1, lax.rem(b + bands - 1, bands))):
            held = lax.rem(b - sign * (hop - 1) + bands, bands)
            got = lax.rem(b - sign * hop + bands, bands)
            if sign > 0:
                sends = jnp.logical_and(b < bands - 1, b >= hop - 1)
                receives = b >= hop
            else:
                sends = jnp.logical_and(b > 0, b + hop - 1 < bands)
                receives = b + hop < bands
            if hop == 1:
                source = pj_hbm.at[:, pl.ds(pl.multiple_of(g * share, share), share), :]
            else:
                source = pw.at[:, share_rows(held, g), :]
            move = remote(source, pw.at[:, share_rows(held, g), :], band=peer)
            pair.append((move, sends, receives, got))
        hops.append(pair)

    def send_hop(index):
        for move, sends, _, _ in hops[index]:
            begin(move, sends)

    def take_hop(index):
        for move, _, receives, got in hops[index]:

            @pl.when(receives)
            def _(move=move):
                move.wait_recv()

        if index + 1 < len(hops):
            send_hop(index + 1)
        for _, _, receives, got in hops[index]:
            onward = pw.at[:, share_rows(got, g), :]
            for peer in part_peers:
                move = remote(onward, onward, groups=peer)
                begin(move, receives)
                passed.append((move, receives))

    send_hop(0)
    for copy in first:
        copy.wait_recv()

    mean, scale = combined(stat_a)
    mine, crossed, sibs, fars = (channel_rows(s) for s in (h, cross, sibling, far))
    for row in range(rows):
        value = normalized(lat_ref[row], mean, scale, column(0), column(1))
        grid_in[row + 1, mine, :] = (value / (1.0 + jnp.exp(-value))).astype(jnp.bfloat16)

    def gather_pieces(buffer, pieces):
        sent = []
        for piece in pieces:
            own = buffer.at[piece, mine, :]
            there = buffer.at[piece, crossed, :]
            sent.append(
                (
                    remote(own, own, head=cross),
                    remote(own, own, head=sibling),
                    remote(there, there, head=sibling),
                )
            )
        return sent

    edges = (pl.ds(rows, 1), pl.ds(1, 1), pl.ds(2, rows - 2))
    gathered = gather_pieces(grid_in, edges)
    below, above = lax.rem(b + 1, bands), lax.rem(b + bands - 1, bands)
    halo = []
    for source, target, peer, sends, receives in (
        (rows, 0, below, b < bands - 1, b > 0),
        (1, rows + 1, above, b > 0, b < bands - 1),
    ):
        for shard in (mine, crossed):
            move = remote(grid_in.at[source, shard, :], grid_in.at[target, shard, :], band=peer)
            onward = grid_in.at[target, shard, :]
            halo.append((move, remote(onward, onward, head=sibling), sends, receives))
    for to_cross, to_sibling, _ in gathered:
        begin(to_cross)
        begin(to_sibling)
    for index in (0, 2):
        move, _, sends, _ = halo[index]
        begin(move, sends)

    for index, (to_cross, _, onward) in enumerate(gathered):
        to_cross.wait_recv()
        begin(onward)
        if index < 2:
            move, _, sends, _ = halo[2 * index + 1]
            begin(move, sends)

    take_hop(0)
    for target, receives in ((0, b > 0), (rows + 1, b < bands - 1)):

        @pl.when(jnp.logical_not(receives))
        def _(target=target):
            grid_in[target] = jnp.zeros((channels, width), jnp.bfloat16)

    for move, onward, _, receives in halo:

        @pl.when(receives)
        def _(move=move):
            move.wait_recv()

        begin(onward, receives)

    for _, to_sibling, onward in gathered:
        to_sibling.wait_recv()
        onward.wait_recv()
    for _, onward, _, receives in halo:

        @pl.when(receives)
        def _(onward=onward):
            onward.wait_recv()

    for index in range(1, min(2, len(hops))):
        take_hop(index)
    load_kernel.wait()
    taps = []
    for beside in range(3):
        summed = None
        for over in range(3):
            window = jnp.concatenate([grid_in[over + row] for row in range(rows)], axis=1)
            part = jnp.dot(kw[over, beside], window, preferred_element_type=jnp.float32)
            summed = part if summed is None else summed + part
        taps.append(summed)
    place = lax.broadcasted_iota(jnp.int32, (local, width), 1)
    bias = column(2)
    for row in range(rows):
        span = slice(row * width, (row + 1) * width)
        left = jnp.where(place == 0, 0.0, pltpu.roll(taps[0][:, span], 1, 1))
        right = jnp.where(place == width - 1, 0.0, pltpu.roll(taps[2][:, span], width - 1, 1))
        value = lat_ref[row].astype(jnp.float32) + bias + (taps[1][:, span] + left + right)
        wide_ref[row] = value
        conv_ref[row] = value.astype(jnp.bfloat16)

    statistics(lambda row: conv_ref[row], stat_b)
    second = exchange(stat_b)
    for copy in second:
        begin(copy)

    for copy in second:
        copy.wait_recv()
    mean, scale = combined(stat_b)
    for row in range(rows):
        value = normalized(conv_ref[row], mean, scale, column(3), column(4))
        norm_in[row, mine, :] = value.astype(jnp.bfloat16)
    normed = gather_pieces(norm_in, (pl.ds(0, rows),))
    for to_cross, to_sibling, onward in normed:
        begin(to_cross)
        begin(to_sibling)
    for index in range(2, len(hops)):
        take_hop(index)
    for to_cross, _, onward in normed:
        to_cross.wait_recv()
        begin(onward)
    load_rows.wait()
    for move, receives in passed:

        @pl.when(receives)
        def _(move=move):
            move.wait_recv()

    for to_cross, to_sibling, onward in normed:
        to_sibling.wait_recv()
        onward.wait_recv()

    features = jnp.concatenate([norm_in[row] for row in range(rows)], axis=1)
    contract_first = lambda left, right: lax.dot_general(
        left, right, (((0,), (0,)), ((), ())), preferred_element_type=jnp.float32
    )
    spread = []
    for kind in range(3):
        made = contract_first(pw[kind], features).astype(jnp.bfloat16)
        for head in range(bands):
            qkv_out[head, kind] = made[head * HEAD_SIZE : (head + 1) * HEAD_SIZE]
        qkv_in[b, kind] = qkv_out[b, kind]
        moves = [
            remote(qkv_out.at[peer, kind], qkv_in.at[b, kind], band=peer) for peer in band_peers
        ]
        for copy in moves:
            begin(copy)
        spread.append(moves)

    inner = bands * HEAD_SIZE
    factor = HEAD_SIZE ** (-0.5) * math.log2(math.e)

    def feature_rows(shard, band):
        return pl.ds(pl.multiple_of(shard * inner + band * HEAD_SIZE, HEAD_SIZE), HEAD_SIZE)

    onwards = [lax.rem(b + step, bands) for step in range(bands)]
    returned = [
        remote(att_out.at[index], att_in.at[feature_rows(h, b), :], band=source)
        for index, source in enumerate(band_sources)
    ]
    final = []
    for source in onwards:
        own = att_in.at[feature_rows(h, source), :]
        there = att_in.at[feature_rows(cross, source), :]
        final.append(
            (
                remote(own, own, head=cross),
                remote(own, own, head=sibling),
                remote(there, there, head=sibling),
            )
        )

    def pass_on(index):
        if index > 0:
            returned[index - 1].wait_recv()
        begin(final[index][0])
        begin(final[index][1])

    def relay(index):
        final[index][0].wait_recv()
        begin(final[index][2])

    for moves in spread[:2]:
        for copy in moves:
            copy.wait_recv()
    keys = jnp.concatenate([qkv_in[source, 1] for source in range(bands)], axis=1).T
    values = None
    for index in list(range(1, bands)) + [0]:
        query = qkv_in[b if index == 0 else band_sources[index - 1], 0]
        scores = jnp.dot(keys, query, preferred_element_type=jnp.float32)
        top = jnp.max(scores, axis=0, keepdims=True)
        heavy = jnp.exp2((scores - top) * factor)
        total = jnp.sum(heavy, axis=0, keepdims=True)
        if values is None:
            for copy in spread[2]:
                copy.wait_recv()
            values = jnp.concatenate([qkv_in[source, 2] for source in range(bands)], axis=1)
        mixed = jnp.dot(values, heavy.astype(jnp.bfloat16), preferred_element_type=jnp.float32)
        result = (mixed / total).astype(jnp.bfloat16)
        if index > 0:
            att_out[index - 1] = result
            begin(returned[index - 1])
            if index > 1:
                pass_on(index - 1)
            if index > 2:
                relay(index - 2)
        else:
            att_in[feature_rows(h, b), :] = result
            pass_on(0)
    pass_on(bands - 1)
    for index in list(range(max(bands - 2, 1), bands)) + [0]:
        relay(index)
    load_output.wait()
    for _, to_sibling, onward in final:
        to_sibling.wait_recv()
        onward.wait_recv()
    outgoing = jnp.dot(ow[...], att_in[...], preferred_element_type=jnp.float32)
    bias = column(5)
    for row in range(rows):
        span = slice(row * width, (row + 1) * width)
        gain_ref[row] = conv_ref[row].astype(jnp.float32) + bias + outgoing[:, span]

    for copy, sends in opened:
        if sends is None:
            copy.wait_send()
        else:

            @pl.when(sends)
            def _(copy=copy):
                copy.wait_send()


def pair_shards(
    parts,
    bands,
    heads,
    latent,
    first_gain,
    first_shift,
    kernel,
    kernel_bias,
    second_gain,
    second_shift,
    projection,
    output_weight,
    output_bias,
):
    rows, width, local = latent.shape
    channels, tokens = local * heads, rows * width
    inner = projection.shape[2]
    groups_here = local // (CHANNELS // NORM_GROUPS)
    vectors = [first_gain, first_shift, kernel_bias, second_gain, second_shift, output_bias]
    gap = jnp.zeros((-local % 128,), jnp.float32)
    flat = jnp.concatenate([piece for vector in vectors for piece in (vector, gap)])
    params = jnp.pad(flat, (0, -flat.shape[0] % 1024)).reshape(-1, 128)
    vmem = pl.BlockSpec(memory_space=pltpu.VMEM)
    hbm = pl.BlockSpec(memory_space=pl.ANY)
    result = jax.ShapeDtypeStruct((rows, local, width), jnp.float32)
    copies = 96
    call = pl.pallas_call(
        functools.partial(pair_kernel, (parts, bands, heads, rows, local, width)),
        out_shape=(result, result),
        in_specs=[vmem, vmem, hbm, hbm, hbm],
        out_specs=(vmem, vmem),
        scratch_shapes=[
            pltpu.VMEM((3, 3, local, channels), jnp.bfloat16),
            pltpu.VMEM((3, channels, inner), jnp.bfloat16),
            pltpu.VMEM((local, inner * heads), jnp.bfloat16),
            pltpu.VMEM((bands, 2, groups_here, width), jnp.float32),
            pltpu.VMEM((bands, 2, groups_here, width), jnp.float32),
            pltpu.VMEM((rows + 2, channels, width), jnp.bfloat16),
            pltpu.VMEM((rows, channels, width), jnp.bfloat16),
            pltpu.VMEM((bands, 3, HEAD_SIZE, tokens), jnp.bfloat16),
            pltpu.VMEM((bands, 3, HEAD_SIZE, tokens), jnp.bfloat16),
            pltpu.VMEM((bands - 1, HEAD_SIZE, tokens), jnp.bfloat16),
            pltpu.VMEM((inner * heads, tokens), jnp.bfloat16),
            pltpu.VMEM((rows, local, width), jnp.bfloat16),
            pltpu.SemaphoreType.DMA((3,)),
            pltpu.SemaphoreType.DMA((copies,)),
            pltpu.SemaphoreType.DMA((copies,)),
        ],
        compiler_params=pltpu.CompilerParams(
            collective_id=0, has_side_effects=True, vmem_limit_bytes=60 << 20
        ),
    )
    wide, gained = call(
        jnp.transpose(latent, (0, 2, 1)),
        params,
        jnp.transpose(kernel, (1, 2, 0, 3)),
        jnp.transpose(projection, (1, 0, 2)),
        output_weight,
    )
    convolved = jnp.transpose(wide, (0, 2, 1)).astype(jnp.bfloat16)
    return convolved, jnp.transpose(gained, (0, 2, 1)).astype(jnp.bfloat16)


def solution(mesh):
    placed = (
        P(("groups", "band"), None, "head"),
        P("head"),
        P("head"),
        P("head", None, None, None),
        P("head"),
        P("head"),
        P("head"),
        P("band", None, "head"),
        P("head", None),
        P("head"),
    )
    parts, bands, heads = (mesh.shape[axis] for axis in ("groups", "band", "head"))
    paired = heads == 4 and bands > 1 and HEADS == heads * bands and CHANNELS % (16 * parts * heads) == 0
    body = functools.partial(pair_shards, parts, bands, heads) if paired else shards
    return jax.shard_map(
        body,
        mesh=mesh,
        in_specs=placed,
        out_specs=(P(("groups", "band"), None, "head"), P(("groups", "band"), None, "head")),
        check_vma=False,
    )
```
